256 devices in a mesh: epoch: 16 (over y, x), sky: 16 (over z, core).
Axes of the slice: x: 4, y: 4, z: 8, core: 2. Of those that a mesh axis runs over, the one named last changes fastest.
Arguments:
- images: float32 [256, 32, 8192], P('epoch', None, 'sky'), may hold values from -6 to 6
- variances: float32 [256, 32, 8192], P('epoch', None, 'sky'), may hold values from 0.25 to 4
- coefficients: bfloat16 [256, 4, 32, 8192], P('epoch', None, None, 'sky'), may hold values from 0.049804688 to 0.5
- row_filters: float32 [256, 4, 11], P('epoch'), may hold values from 0.03 to 0.3
- col_filters: float32 [256, 4, 11], P('epoch'), may hold values from 0.03 to 0.3
- dithers: int32 [256, 2], P('epoch'), may hold values from -3 to 3
Outputs:
- template: float32 [32, 8192], P(None, 'sky')
- mean_weight: float32 [32, 8192], P(None, 'sky')
The draws below stay inside these ranges and needn't reach their ends.
All inputs are finite; a program needn't handle non-finite values.
Results may differ from the reference program's by a relative error of at most 0.0003.
Values sent between devices are 32-bit elements; how exact they have to be, the bound alone decides.
A program may use at most 128 MiB of HBM per device.

```python
import math
import jax
import jax.numpy as jnp
from jax import lax

ROWS = 32
TAPS = 11
BASES = 4
REJECT = 4
MAXDITHER = 3
HALF = 5
HALO = 8
EPOCHS = 256
COLUMNS = 8192


def shared_dithers(key):
    base_key = jax.random.fold_in(key, 7)
    span_count = 2 * MAXDITHER + 1
    row_order = jax.random.permutation(jax.random.fold_in(base_key, 1), EPOCHS)
    col_order = jax.random.permutation(jax.random.fold_in(base_key, 2), EPOCHS)
    return jnp.stack([row_order % span_count - MAXDITHER, col_order % span_count - MAXDITHER], axis=1).astype(jnp.int32)


def draw_dithers(key, part):
    return shared_dithers(key)


def draw_images(key, part):
    shifts = shared_dithers(key)
    sky_shape = (ROWS + 2 * MAXDITHER, COLUMNS + 2 * MAXDITHER)
    sky_plane = jnp.clip(jax.random.normal(jax.random.fold_in(key, 31), sky_shape, jnp.float32), -4.0, 4.0)
    noise_plane = 0.5 * jnp.clip(jax.random.normal(jax.random.fold_in(key, 32), (EPOCHS, ROWS, COLUMNS), jnp.float32), -4.0, 4.0)

    def place_epoch(offsets):
        return lax.dynamic_slice(sky_plane, (offsets[0] + MAXDITHER, offsets[1] + MAXDITHER), (ROWS, COLUMNS))
    return (jax.vmap(place_epoch)(shifts) + noise_plane).astype(jnp.float32)


def block_scale(key, shape, cuts, smallest, top_value):
    def one(position, shards_of):
        draws = jax.random.uniform(jax.random.fold_in(jax.random.fold_in(key, 6), position), (shards_of,), jnp.float32, smallest / len(cuts), top_value / len(cuts))
        return jnp.repeat(jnp.exp(draws), shape[position] // shards_of).reshape((-1,) + (1,) * (len(shape) - position - 1))

    level = one(*cuts[0])
    for cut in cuts[1:]:
        level = level * one(*cut)
    return level


def setup_inputs(seed: int = 0) -> dict:
    streams_of = jax.random.split(jax.random.key(seed), 7)
    images = draw_images(jax.random.fold_in(streams_of[6], 71), 0)
    variances = jnp.clip(jnp.exp(math.log(4.0) - 2.7725887 * jax.random.uniform(streams_of[1], (EPOCHS, ROWS, COLUMNS), jnp.float32) ** block_scale(streams_of[1], (EPOCHS, ROWS, COLUMNS), ((0, 16), (2, 16)), -0.2, 0.2)), 0.25, 4.0)
    coefficients = jnp.clip(jnp.exp(math.log(0.5) - 2.306499 * jax.random.uniform(streams_of[2], (EPOCHS, BASES, ROWS, COLUMNS), jnp.float32) ** block_scale(streams_of[2], (EPOCHS, BASES, ROWS, COLUMNS), ((0, 16), (3, 16)), -0.2, 0.2)), 0.049804688, 0.5).astype(jnp.bfloat16)
    row_filters = jnp.clip(jnp.exp(math.log(0.3) - 2.3025852 * jax.random.uniform(streams_of[3], (EPOCHS, BASES, TAPS), jnp.float32) ** block_scale(streams_of[3], (EPOCHS, BASES, TAPS), ((0, 16),), -0.2, 0.2)), 0.03, 0.3)
    col_filters = jnp.clip(jnp.exp(math.log(0.3) - 2.3025852 * jax.random.uniform(streams_of[4], (EPOCHS, BASES, TAPS), jnp.float32) ** block_scale(streams_of[4], (EPOCHS, BASES, TAPS), ((0, 16),), -0.2, 0.2)), 0.03, 0.3)
    dithers = draw_dithers(jax.random.fold_in(streams_of[6], 71), 0)
    return dict(images=images, variances=variances, coefficients=coefficients, row_filters=row_filters, col_filters=col_filters, dithers=dithers)


READ_NOISE = 0.25


def smear_field(field, shifts, row_taps, col_taps, coeff_plane):
    band_rows, strip_cols = field.shape
    padded = jnp.pad(field, HALO)
    first_row = (HALO - HALF - shifts[0]).astype(jnp.int32)
    first_col = (HALO - HALF - shifts[1]).astype(jnp.int32)
    window = lax.dynamic_slice(padded, (first_row, first_col), (band_rows + 2 * HALF, strip_cols + 2 * HALF))
    row_pass = row_taps[:, 0, None, None] * window[None, 0:band_rows, :]
    for offset in range(1, TAPS):
        row_pass = row_pass + row_taps[:, offset, None, None] * window[None, offset:offset + band_rows, :]
    col_pass = col_taps[:, 0, None, None] * row_pass[:, :, 0:strip_cols]
    for offset in range(1, TAPS):
        col_pass = col_pass + col_taps[:, offset, None, None] * row_pass[:, :, offset:offset + strip_cols]
    return jnp.sum(coeff_plane.astype(jnp.float32) * col_pass, axis=0)


def reference(images, variances, coefficients, row_filters, col_filters, dithers):
    def one_epoch(pieces):
        image_plane, variance_plane, coeff_plane, row_taps, col_taps, shifts = pieces
        smeared_image = smear_field(image_plane, shifts, row_taps, col_taps, coeff_plane)
        smeared_variance = smear_field(variance_plane, shifts, row_taps, col_taps, coeff_plane)
        weight = 1.0 / (smeared_variance + READ_NOISE)
        return weight * smeared_image, weight

    weighted, weights = lax.map(one_epoch, (images, variances, coefficients, row_filters, col_filters, dithers))

    def trimmed_sum(stacked_values):
        ordered = jnp.sort(stacked_values, axis=0)
        return jnp.sum(stacked_values, axis=0) - jnp.sum(ordered[:REJECT], axis=0) - jnp.sum(ordered[EPOCHS - REJECT:], axis=0)

    numerator = trimmed_sum(weighted)
    denominator = trimmed_sum(weights)
    return numerator / denominator, denominator / (EPOCHS - 2 * REJECT)
```

```python
import jax
import jax.numpy as jnp
from jax import lax
from jax.experimental import pallas as pl
from jax.experimental.pallas import tpu as pltpu
from jax.sharding import PartitionSpec as P

TAPS = 11
BASES = 4
REJECT = 4
HALF = 5
HALO = 8
READ_NOISE = 0.25

LANES = 128
EPOCHS = 16
ROWS = 32
BLOCKS = 4
SIDE = 4
PEERS = SIDE * SIDE
LISTS = 2 * (2 * REJECT + 1)
GROUPS = ((1, 2), (0, 3))
MESH = pl.DeviceIdType.MESH


def split(value):
    high = value.astype(jnp.bfloat16)
    return high, value - high.astype(jnp.float32)


def exchange(first, second):
    return jnp.minimum(first, second), jnp.maximum(first, second)


def sort_four(values):
    a, b, c, d = values
    a, b = exchange(a, b)
    c, d = exchange(c, d)
    a, c = exchange(a, c)
    b, d = exchange(b, d)
    b, c = exchange(b, c)
    return [a, b, c, d]


def sort_bitonic(values):
    a, b, c, d = values
    a, c = exchange(a, c)
    b, d = exchange(b, d)
    a, b = exchange(a, b)
    c, d = exchange(c, d)
    return [a, b, c, d]


def lower_four(first, second):
    return [jnp.minimum(first[i], second[REJECT - 1 - i]) for i in range(REJECT)]


def upper_four(first, second):
    return [jnp.maximum(first[i], second[REJECT - 1 - i]) for i in range(REJECT)]


def merge_ends(first, second, last=False):
    low = lower_four(first[0], second[0])
    high = upper_four(first[1], second[1])
    if not last:
        low, high = sort_bitonic(low), sort_bitonic(high)
    return low, high


def merge_tree(lists):
    while len(lists) > 1:
        last = False
        lists = [merge_ends(lists[i], lists[i + 1], last) for i in range(0, len(lists), 2)]
    return lists[0]


def sum_tree(values):
    values = list(values)
    while len(values) > 1:
        values = [values[i] + values[i + 1] for i in range(0, len(values) - 1, 2)] + (
            [values[-1]] if len(values) % 2 else []
        )
    return values[0]


def kernel(
    img_hbm, var_hbm, coef_hbm, rowf_ref, colf_ref, dith_ref, out_ref,
    img, var, coef, filt, flip, toep, band, pack, halo, val, lists, stage1, mid, stage2, final,
    in_sem, halo_send, halo_recv, s1_send, s1_recv, s2_send, s2_recv, own_sem, fin_send, fin_recv,
):
    me = lax.axis_index("epoch")
    sky = lax.axis_index("sky")
    strips = lax.axis_size("sky")
    my_y, my_x = me // SIDE, me % SIDE
    right, left = (sky + 1) % strips, (sky + strips - 1) % strips

    def peer_at(dy, dx):
        return ((my_y + dy) % SIDE) * SIDE + (my_x + dx) % SIDE

    offsets = [(dy, dx) for dy in range(SIDE) for dx in range(SIDE) if dy or dx]

    barrier = pltpu.get_barrier_semaphore()
    for neighbour in (left, right):
        pl.semaphore_signal(barrier, inc=1, device_id=(me, neighbour), device_id_type=MESH)
    for dy, dx in offsets:
        pl.semaphore_signal(barrier, inc=1, device_id=(peer_at(dy, dx), sky), device_id_type=MESH)

    loads = [
        pltpu.make_async_copy(img_hbm, img, in_sem.at[0]),
        pltpu.make_async_copy(var_hbm, var, in_sem.at[1]),
        pltpu.make_async_copy(coef_hbm, coef, in_sem.at[2]),
    ]
    for load in loads:
        load.start()

    lane8 = lax.broadcasted_iota(jnp.int32, (ROWS, LANES), 1)
    filt[...] = jnp.zeros_like(filt)
    for e in range(EPOCHS):
        filt[0, BASES * e : BASES * (e + 1), 0:TAPS] = rowf_ref[e]
        filt[1, BASES * e : BASES * (e + 1), 0:TAPS] = colf_ref[e]
    tap = lax.broadcasted_iota(jnp.int32, (LANES, LANES), 0)
    place = lax.broadcasted_iota(jnp.int32, (LANES, LANES), 1)
    count = EPOCHS * BASES
    for kind in range(2):
        high, low = split(filt[kind])
        parts = jnp.concatenate([high, low.astype(jnp.bfloat16)], axis=0)
        for turn in range(8):
            target = tap + turn if kind == 0 else TAPS - 1 - tap + turn
            moved = jnp.dot(
                parts,
                jnp.where(place == target, 1.0, 0.0).astype(jnp.bfloat16),
                preferred_element_type=jnp.float32,
            )
            flip[2 * kind, pl.ds(turn, count, stride=8), :] = moved[0:count]
            flip[2 * kind + 1, pl.ds(turn, count, stride=8), :] = moved[count : 2 * count]

    keep = place <= tap
    tail_keep = (place > tap)[0:16]

    def build(e, _):
        row_turn = LANES - HALF - dith_ref[e, 0]
        col_turn = LANES - HALF - HALO + dith_ref[e, 1]
        pad = jnp.zeros((LANES - 48, LANES), jnp.bfloat16)
        for b in range(BASES):
            at = e * BASES + b
            cols = slice(b * LANES, (b + 1) * LANES)

            def turned(which, rows, turn):
                base = flip[which, pl.ds(pl.multiple_of(at * 8, 8), 8), :]
                return jnp.concatenate(
                    [pltpu.roll(base, (turn + g) % LANES, 1) for g in range(0, rows, 8)], axis=0
                )

            high = jnp.where(lane8 < ROWS, turned(0, ROWS, row_turn), 0.0)
            low = jnp.where(lane8 < ROWS, turned(1, ROWS, row_turn), 0.0)
            both = high + pltpu.roll(high, ROWS, 1) + pltpu.roll(low, 2 * ROWS, 1)
            band[e, b] = both.astype(jnp.bfloat16)

            high = turned(2, LANES, col_turn)
            low = turned(3, LANES, col_turn)
            top = jnp.where(keep, high, 0.0).astype(jnp.bfloat16)
            toep[e, 0:LANES, cols] = top
            toep[e, LANES : 2 * LANES, cols] = top
            toep[e, 2 * LANES : 3 * LANES, cols] = jnp.where(keep, low, 0.0).astype(jnp.bfloat16)
            tail = jnp.where(tail_keep, high[0:16], 0.0).astype(jnp.bfloat16)
            toep[e, 3 * LANES : 3 * LANES + 16, cols] = tail
            toep[e, 3 * LANES + 16 : 3 * LANES + 32, cols] = tail
            toep[e, 3 * LANES + 32 : 3 * LANES + 48, cols] = jnp.where(
                tail_keep, low[0:16], 0.0
            ).astype(jnp.bfloat16)
            toep[e, 3 * LANES + 48 : 4 * LANES, cols] = pad
        return 0

    loads[0].wait()
    loads[1].wait()
    fields = (img, var)
    last_cols = slice((BLOCKS - 1) * LANES, BLOCKS * LANES)

    def gather_edges(e, _):
        mine = (lane8 >= HALO * e) & (lane8 < HALO * (e + 1))
        for f in range(2):
            first = pltpu.roll(fields[f][e, :, 0:LANES], HALO * e, 1)
            last = pltpu.roll(fields[f][e, :, last_cols], (HALO * e + HALO) % LANES, 1)
            pack[0, f] = jnp.where(mine, first, pack[0, f])
            pack[1, f] = jnp.where(mine, last, pack[1, f])
        return 0

    lax.fori_loop(0, EPOCHS, gather_edges, 0)

    pl.semaphore_wait(barrier, 2 + len(offsets))
    halo_copies = []
    for side, target in ((0, left), (1, right)):
        copy = pltpu.make_async_remote_copy(
            src_ref=pack.at[side],
            dst_ref=halo.at[side],
            send_sem=halo_send.at[side],
            recv_sem=halo_recv.at[side],
            device_id=(me, target),
            device_id_type=MESH,
        )
        copy.start()
        halo_copies.append(copy)

    lax.fori_loop(0, EPOCHS, build, 0)

    def shifted(field, e, tile):
        def at(t):
            return pltpu.roll(field[e, :, t * LANES : (t + 1) * LANES], HALO, 1)

        f = 0 if field is img else 1
        if tile == 0:
            before = pltpu.roll(halo[1, f], (LANES - HALO * e) % LANES, 1) * jnp.where(
                sky == 0, 0.0, 1.0
            )
        else:
            before = at(tile - 1)
        if tile == BLOCKS:
            here = pltpu.roll(halo[0, f], (LANES + HALO - HALO * e) % LANES, 1) * jnp.where(
                sky == strips - 1, 0.0, 1.0
            )
        else:
            here = at(tile)
        return jnp.where(lane8 < HALO, before, here)

    def smear(blocks, e):
        left_rows = []
        for k in blocks:
            for field in fields:
                main_high, main_low = split(shifted(field, e, k))
                tail_high, tail_low = split(shifted(field, e, k + 1))
                tail_high = tail_high.astype(jnp.float32)
                tail = jnp.where(
                    lane8 < 16,
                    tail_high,
                    jnp.where(
                        lane8 < 32,
                        pltpu.roll(tail_low, 16, 1),
                        jnp.where(lane8 < 48, pltpu.roll(tail_high, 32, 1), 0.0),
                    ),
                )
                left_rows.append(
                    jnp.concatenate(
                        [main_high, main_low.astype(jnp.bfloat16), main_high, tail.astype(jnp.bfloat16)],
                        axis=1,
                    )
                )
        left_side = jnp.concatenate(left_rows, axis=0)
        spread = jnp.dot(left_side, toep[e], preferred_element_type=jnp.float32)
        spread_high, spread_low = split(spread)
        spread_low = spread_low.astype(jnp.bfloat16)
        count = 2 * len(blocks)

        def along(part, b):
            return jnp.concatenate(
                [part[i * ROWS : (i + 1) * ROWS, b * LANES : (b + 1) * LANES] for i in range(count)],
                axis=1,
            )

        total = None
        for b in range(BASES):
            high = along(spread_high, b)
            stacked = jnp.concatenate([high, along(spread_low, b), high], axis=0)
            smeared = jnp.dot(band[e, b][:, 0 : 3 * ROWS], stacked, preferred_element_type=jnp.float32)
            planes = []
            for k in blocks:
                plane = coef[e, b, :, k * LANES : (k + 1) * LANES].astype(jnp.float32)
                planes += [plane, plane]
            term = smeared * jnp.concatenate(planes, axis=1)
            total = term if total is None else total + term
        for i, k in enumerate(blocks):
            image = total[:, 2 * i * LANES : (2 * i + 1) * LANES]
            variance = total[:, (2 * i + 1) * LANES : (2 * i + 2) * LANES]
            weight = 1.0 / (variance + READ_NOISE)
            val[k, 0, e] = weight * image
            val[k, 1, e] = weight
        return 0

    def select(k, index, _):
        f, rows = index // (ROWS // 8), pl.ds(pl.multiple_of(index % (ROWS // 8) * 8, 8), 8)
        values = [val[k, f, e, rows, :] for e in range(EPOCHS)]
        sorts = [sort_four(values[i : i + 4]) for i in range(0, EPOCHS, 4)]
        pairs = []
        for i in (0, 2):
            pairs.append(
                (
                    sort_bitonic(lower_four(sorts[i], sorts[i + 1])),
                    sort_bitonic(upper_four(sorts[i], sorts[i + 1])),
                )
            )
        low, high = merge_ends(pairs[0], pairs[1])
        ends = low + high + [sum_tree(values)]
        for place, value in enumerate(ends):
            lists[k, f * (LISTS // 2) + place, rows, :] = value
        return 0

    def merge(pieces, last):
        result = []
        for f in range(2):
            base = f * (LISTS // 2)
            ends = []
            for piece in pieces:
                ends.append(
                    (
                        [piece(base + i) for i in range(REJECT)],
                        [piece(base + REJECT + i) for i in range(REJECT)],
                    )
                )
            low, high = merge_tree(ends)
            total = sum_tree([piece(base + 2 * REJECT) for piece in pieces])
            result.append((low, high, total))
        return result

    def first_axis(k):
        return k % 2

    def along_axis(axis, step):
        return peer_at(0, step) if axis == 0 else peer_at(step, 0)

    def place_on(axis, step):
        return (my_x + step) % SIDE if axis == 0 else (my_y + step) % SIDE

    def send_first(k):
        copies = []
        axis = first_axis(k)
        for step in range(1, SIDE):
            rows = pl.ds(pl.multiple_of(place_on(axis, step) * 8, 8), 8)
            copy = pltpu.make_async_remote_copy(
                src_ref=lists.at[k, :, rows, :],
                dst_ref=stage1.at[k, step - 1],
                send_sem=s1_send.at[k, step - 1],
                recv_sem=s1_recv.at[k, step - 1],
                device_id=(along_axis(axis, step), sky),
                device_id_type=MESH,
            )
            copy.start()
            copies.append(copy)
        return copies

    def send_second(k, copies):
        axis = first_axis(k)
        for copy in copies:
            copy.wait_recv()
        rows = pl.ds(pl.multiple_of(place_on(axis, 0) * 8, 8), 8)
        pieces = [lambda i: lists[k, i, rows, :]]
        for step in range(1, SIDE):
            pieces.append(lambda i, step=step: stage1[k, step - 1, i])
        for f, (low, high, total) in enumerate(merge(pieces, False)):
            for place, value in enumerate(low + high + [total]):
                mid[k, f * (LISTS // 2) + place] = value
        axis = 1 - axis
        own = pltpu.make_async_copy(
            mid.at[k, :, pl.ds(place_on(axis, 0) * 2, 2), :],
            stage2.at[0, :, pl.ds(2 * k, 2), :],
            own_sem.at[k],
        )
        own.start()
        result = []
        for step in range(1, SIDE):
            copy = pltpu.make_async_remote_copy(
                src_ref=mid.at[k, :, pl.ds(place_on(axis, step) * 2, 2), :],
                dst_ref=stage2.at[step, :, pl.ds(2 * k, 2), :],
                send_sem=s2_send.at[k, step - 1],
                recv_sem=s2_recv.at[k, step - 1],
                device_id=(along_axis(axis, step), sky),
                device_id_type=MESH,
            )
            copy.start()
            result.append(copy)
        return own, result

    firsts, seconds = {}, {}
    loads[2].wait()
    for number, blocks in enumerate(GROUPS):
        if number == 1:
            for copy in halo_copies:
                copy.wait_recv()
        lax.fori_loop(0, EPOCHS, lambda e, _: smear(blocks, e), 0)
        for k in blocks:
            lax.fori_loop(0, 2 * (ROWS // 8), lambda index, _: select(k, index, _), 0)
            firsts[k] = send_first(k)
    for blocks in GROUPS:
        for k in blocks:
            seconds[k] = send_second(k, firsts[k])
    for own, copies in seconds.values():
        own.wait()
        for copy in copies:
            copy.wait_recv()

    pieces = [lambda i, step=step: stage2[step, i] for step in range(SIDE)]
    for f, (low, high, total) in enumerate(merge(pieces, True)):
        final[me, f] = total - sum_tree(low) - sum_tree(high)
    copies = []
    for i, (dy, dx) in enumerate(offsets):
        copy = pltpu.make_async_remote_copy(
            src_ref=final.at[me],
            dst_ref=final.at[me],
            send_sem=fin_send.at[i],
            recv_sem=fin_recv.at[i],
            device_id=(peer_at(dy, dx), sky),
            device_id_type=MESH,
        )
        copy.start()
        copies.append(copy)
    for i, (dy, dx) in enumerate(offsets):
        source = peer_at(SIDE - dy, SIDE - dx)
        pltpu.make_async_remote_copy(
            src_ref=final.at[source],
            dst_ref=final.at[source],
            send_sem=fin_send.at[i],
            recv_sem=fin_recv.at[i],
            device_id=(source, sky),
            device_id_type=MESH,
        ).wait_recv()

    for k in range(BLOCKS):
        for outer in range(SIDE):
            for f in range(2):
                parts = []
                for inner in range(SIDE):
                    owner = inner * SIDE + outer if first_axis(k) == 0 else outer * SIDE + inner
                    parts.append(final[owner, f, 2 * k : 2 * k + 2, :])
                out_ref[f, outer * 8 : outer * 8 + 8, k * LANES : (k + 1) * LANES] = jnp.concatenate(
                    parts, axis=0
                )

    for copy in halo_copies:
        copy.wait_send()
    for k in range(BLOCKS):
        for copy in firsts[k] + seconds[k][1]:
            copy.wait_send()
    for copy in copies:
        copy.wait_send()


def per_device(images, variances, coefficients, row_filters, col_filters, dithers):
    f32, bf16 = jnp.float32, jnp.bfloat16
    dma = pltpu.SemaphoreType.DMA
    whole = pl.BlockSpec(memory_space=pltpu.VMEM)
    trimmed = pl.pallas_call(
        kernel,
        out_shape=jax.ShapeDtypeStruct((2, ROWS, BLOCKS * LANES), f32),
        in_specs=[pl.BlockSpec(memory_space=pl.ANY)] * 3
        + [whole, whole, pl.BlockSpec(memory_space=pltpu.SMEM)],
        out_specs=whole,
        scratch_shapes=[
            pltpu.VMEM((EPOCHS, ROWS, BLOCKS * LANES), f32),
            pltpu.VMEM((EPOCHS, ROWS, BLOCKS * LANES), f32),
            pltpu.VMEM((EPOCHS, BASES, ROWS, BLOCKS * LANES), bf16),
            pltpu.VMEM((2, EPOCHS * BASES, LANES), f32),
            pltpu.VMEM((4, EPOCHS * BASES * 8, LANES), f32),
            pltpu.VMEM((EPOCHS, 4 * LANES, BASES * LANES), bf16),
            pltpu.VMEM((EPOCHS, BASES, ROWS, LANES), bf16),
            pltpu.VMEM((2, 2, ROWS, LANES), f32),
            pltpu.VMEM((2, 2, ROWS, LANES), f32),
            pltpu.VMEM((BLOCKS, 2, EPOCHS, ROWS, LANES), f32),
            pltpu.VMEM((BLOCKS, LISTS, ROWS, LANES), f32),
            pltpu.VMEM((BLOCKS, SIDE - 1, LISTS, 8, LANES), f32),
            pltpu.VMEM((BLOCKS, LISTS, 8, LANES), f32),
            pltpu.VMEM((SIDE, LISTS, 8, LANES), f32),
            pltpu.VMEM((PEERS, 2, 8, LANES), f32),
            dma((3,)),
            dma((2,)),
            dma((2,)),
            dma((BLOCKS, SIDE - 1)),
            dma((BLOCKS, SIDE - 1)),
            dma((BLOCKS, SIDE - 1)),
            dma((BLOCKS, SIDE - 1)),
            dma((BLOCKS,)),
            dma((PEERS - 1,)),
            dma((PEERS - 1,)),
        ],
        compiler_params=pltpu.CompilerParams(
            collective_id=0, has_side_effects=True, vmem_limit_bytes=48 * 1024 * 1024
        ),
        name="coadd",
    )(images, variances, coefficients, row_filters, col_filters, dithers)
    kept_count = float(EPOCHS * lax.axis_size("epoch") - 2 * REJECT)
    return trimmed[0] / trimmed[1], trimmed[1] / kept_count


def solution(mesh):
    placed = (
        P("epoch", None, "sky"),
        P("epoch", None, "sky"),
        P("epoch", None, None, "sky"),
        P("epoch", None, None),
        P("epoch", None, None),
        P("epoch", None),
    )
    return jax.shard_map(
        per_device,
        mesh=mesh,
        in_specs=placed,
        out_specs=(P(None, "sky"), P(None, "sky")),
        check_vma=False,
    )
```

```python
import jax
import jax.numpy as jnp
from jax import lax
from jax.experimental import pallas as pl
from jax.experimental.pallas import tpu as pltpu
from jax.sharding import PartitionSpec as P

TAPS = 11
BASES = 4
REJECT = 4
HALF = 5
HALO = 8
READ_NOISE = 0.25

LANES = 128
EPOCHS = 16
ROWS = 32
BLOCKS = 4
SIDE = 4
PEERS = SIDE * SIDE
LISTS = 2 * REJECT + 1
HALVES = ((1, 2), (0, 3))
OWNER_ROWS = 8
MESH = pl.DeviceIdType.MESH


def split(value):
    high = value.astype(jnp.bfloat16)
    return high, value - high.astype(jnp.float32)


def exchange(first, second):
    return jnp.minimum(first, second), jnp.maximum(first, second)


def sort_four(values):
    a, b, c, d = values
    a, b = exchange(a, b)
    c, d = exchange(c, d)
    a, c = exchange(a, c)
    b, d = exchange(b, d)
    b, c = exchange(b, c)
    return [a, b, c, d]


def sort_bitonic(values):
    a, b, c, d = values
    a, c = exchange(a, c)
    b, d = exchange(b, d)
    a, b = exchange(a, b)
    c, d = exchange(c, d)
    return [a, b, c, d]


def lower_four(first, second):
    return [jnp.minimum(first[i], second[REJECT - 1 - i]) for i in range(REJECT)]


def upper_four(first, second):
    return [jnp.maximum(first[i], second[REJECT - 1 - i]) for i in range(REJECT)]


def merge_ends(first, second, last=False):
    low = lower_four(first[0], second[0])
    high = upper_four(first[1], second[1])
    if not last:
        low, high = sort_bitonic(low), sort_bitonic(high)
    return low, high


def sum_tree(values):
    values = list(values)
    while len(values) > 1:
        values = [values[i] + values[i + 1] for i in range(0, len(values) - 1, 2)] + (
            [values[-1]] if len(values) % 2 else []
        )
    return values[0]


def kernel(
    img_hbm, var_hbm, coef_hbm, rowf_hbm, colf_hbm, dith_hbm, out_ref,
    img, var, coef, rowf, colf, dith, filt, base, spread_high, spread_low, spread_tail, band, ext_high, ext_low, ext_tail,
    spread_high1, spread_low1, spread_tail1, band1, ext_high1, ext_low1, ext_tail1, pack, halo, edge, col0, col1, val, lists,
    near_low, near_high, mid_low, mid_high, far_low, far_high, final,
    in_sem, halo_send, halo_recv, near_send, near_recv, far_send, far_recv, fin_send, fin_recv,
):
    f32, bf16 = jnp.float32, jnp.bfloat16
    pairs = (
        (spread_high, spread_low, spread_tail, band, ext_high, ext_low, ext_tail),
        (spread_high1, spread_low1, spread_tail1, band1, ext_high1, ext_low1, ext_tail1),
    )
    me = lax.axis_index("epoch")
    sky = lax.axis_index("sky")
    strips = lax.axis_size("sky")
    my_y, my_x = me // SIDE, me % SIDE
    right, left = (sky + 1) % strips, (sky + strips - 1) % strips

    def peer_at(dy, dx):
        return ((my_y + dy) % SIDE) * SIDE + (my_x + dx) % SIDE

    offsets = [(dy, dx) for dy in range(SIDE) for dx in range(SIDE) if dy or dx]

    loads = [
        pltpu.make_async_copy(source, target, in_sem.at[i])
        for i, (source, target) in enumerate(
            (
                (rowf_hbm, rowf),
                (colf_hbm, colf),
                (dith_hbm, dith),
                (img_hbm, img),
                (var_hbm, var),
                (coef_hbm, coef),
            )
        )
    ]
    for load in loads:
        load.start()

    barrier = pltpu.get_barrier_semaphore()
    for neighbour in (left, right):
        pl.semaphore_signal(barrier, inc=1, device_id=(me, neighbour), device_id_type=MESH)
    for dy, dx in offsets:
        pl.semaphore_signal(barrier, inc=1, device_id=(peer_at(dy, dx), sky), device_id_type=MESH)

    lane = lax.broadcasted_iota(jnp.int32, (ROWS, LANES), 1)
    lane16 = lane[0:16]

    def within(start, stop, like=lane):
        return jnp.where((like >= start) & (like < stop), 1.0, 0.0).astype(bf16)

    filt[...] = jnp.zeros_like(filt)
    loads[0].wait()
    loads[1].wait()
    for j in range(TAPS):
        for b in range(BASES):
            filt[16 * b + j, 0:EPOCHS] = rowf[j, b, :]
            filt[64 + 16 * b + TAPS - 1 - j, 0:EPOCHS] = colf[j, b, :]
    turned = jnp.transpose(filt[...])[0:EPOCHS]
    for kind in range(2):
        for b in range(BASES):
            at = 16 * (BASES * kind + b)
            taps = pltpu.roll(turned, LANES - at, 1) if at else turned
            taps = jnp.where(lane16 < 16, taps, 0.0)
            high, low = split(taps)
            for part, value in enumerate((high.astype(f32), low.astype(bf16).astype(f32))):
                for turn in range(8):
                    rows = pl.ds(b * EPOCHS * 8 + turn, EPOCHS, stride=8)
                    base[2 * kind + part, rows, :] = pltpu.roll(value, turn, 1) if turn else value

    loads[3].wait()
    loads[4].wait()
    fields = (img, var)
    last_cols = slice((BLOCKS - 1) * LANES, BLOCKS * LANES)

    def gather_edges(e, _):
        mine = (lane >= HALO * e) & (lane < HALO * (e + 1))
        for f in range(2):
            first = pltpu.roll(fields[f][e, :, 0:LANES], HALO * e, 1)
            last = pltpu.roll(fields[f][e, :, last_cols], (HALO * e + HALO) % LANES, 1)
            pack[0, f] = jnp.where(mine, first, pack[0, f])
            pack[1, f] = jnp.where(mine, last, pack[1, f])
        return 0

    lax.fori_loop(0, EPOCHS, gather_edges, 0, unroll=4)

    pl.semaphore_wait(barrier, 2 + len(offsets))
    halo_copies = []
    for side, target in ((0, left), (1, right)):
        copy = pltpu.make_async_remote_copy(
            src_ref=pack.at[side],
            dst_ref=halo.at[side],
            send_sem=halo_send.at[side],
            recv_sem=halo_recv.at[side],
            device_id=(me, target),
            device_id_type=MESH,
        )
        copy.start()
        halo_copies.append(copy)

    loads[2].wait()

    def build(parity, n):
        spread_high, spread_low, spread_tail, band = pairs[parity][0:4]
        e = 2 * n + parity
        row_turn, col_turn = 8 - dith[0, e], dith[1, e]
        for b in range(BASES):
            at = pl.ds(pl.multiple_of((b * EPOCHS + e) * 8, 8), 8)

            def sixteen(which):
                eight = base[which, at, :]
                return jnp.concatenate([eight, pltpu.roll(eight, 8, 1)], axis=0).astype(bf16)

            high, low = sixteen(0), sixteen(1)
            for g in range(2):
                turn = row_turn + (16 * g - HALF - 8) % LANES
                main = pltpu.roll(high, turn, 1) * within(0, ROWS, lane16)
                rest = pltpu.roll(low, turn, 1) * within(0, ROWS, lane16)
                band[n, b, 16 * g : 16 * g + 16, :] = (
                    main + pltpu.roll(main, ROWS, 1) + pltpu.roll(rest, 2 * ROWS, 1)
                )
            tails = []
            for which, target in ((2, spread_high), (3, spread_low)):
                taps = sixteen(which)
                for g in range(8):
                    value = pltpu.roll(taps, col_turn + (16 * g - 13) % LANES, 1)
                    if g == 0:
                        tails.append(value * within(64, LANES, lane16))
                        value = value * within(0, 64, lane16)
                    target[n, b, 16 * g : 16 * g + 16, :] = value
            spread_tail[n, b] = jnp.concatenate([tails[0], tails[0], tails[1]], axis=0)

    def extend(parity, n):
        ext_high, ext_low, ext_tail = pairs[parity][4:7]
        e = 2 * n + parity
        for f in range(2):
            highs, lows = [], []
            for t in range(BLOCKS):
                high, low = split(fields[f][e, :, t * LANES : (t + 1) * LANES])
                highs.append(pltpu.roll(high, HALO, 1))
                lows.append(pltpu.roll(low.astype(bf16), HALO, 1))

            def tile(parts, t):
                value = 0
                if t > 0:
                    value = parts[t - 1] * within(0, HALO)
                if t < BLOCKS:
                    value = value + parts[t] * within(HALO, LANES)
                return value

            highs = [tile(highs, t) for t in range(BLOCKS + 1)]
            lows = [tile(lows, t) for t in range(BLOCKS + 1)]
            for t in range(BLOCKS):
                ext_high[n, f, t] = highs[t]
                ext_low[n, f, t] = lows[t]
                ext_tail[n, f, t] = (
                    highs[t + 1] * within(0, 16)
                    + pltpu.roll(lows[t + 1], 16, 1) * within(16, 32)
                    + pltpu.roll(highs[t + 1], 32, 1) * within(32, 48)
                )

    def spread(half, parity, n, target):
        spread_high, spread_low, spread_tail, _, ext_high, ext_low, ext_tail = pairs[parity]
        e = 2 * n + parity
        highs, lows, tails = [], [], []
        for f in range(2):
            for k in HALVES[half]:
                high, low, tail = ext_high[n, f, k], ext_low[n, f, k], ext_tail[n, f, k]
                if k == 0:
                    turn = (LANES - HALO * e) % LANES
                    high = high + pltpu.roll(edge[0, 0, f], turn, 1) * within(0, HALO)
                    low = low + pltpu.roll(edge[0, 1, f], turn, 1) * within(0, HALO)
                if k == BLOCKS - 1:
                    for part, to in ((0, 8), (1, 24), (0, 40)):
                        turn = (LANES + to - HALO * e) % LANES
                        tail = tail + pltpu.roll(edge[1, part, f], turn, 1) * within(to, to + HALO)
                highs.append(high)
                lows.append(low)
                tails.append(tail)
        highs, lows, tails = (jnp.concatenate(parts, axis=0) for parts in (highs, lows, tails))
        data = jnp.concatenate([highs, lows, highs, tails], axis=1)
        cols = []
        for b in range(BASES):
            high = spread_high[n, b]
            cols.append(jnp.concatenate([high, high, spread_low[n, b], spread_tail[n, b]], axis=0))
        taps = jnp.concatenate(cols, axis=1)
        result = jnp.dot(data[:, 0 : taps.shape[0]], taps, preferred_element_type=f32)
        high, low = split(result)
        low = low.astype(bf16)
        for b in range(BASES):
            for i in range(4):
                rows, lanes = slice(i * ROWS, (i + 1) * ROWS), slice(b * LANES, (b + 1) * LANES)
                target[0, b, i] = high[rows, lanes]
                target[1, b, i] = low[rows, lanes]

    def finish(half, parity, n, source):
        band = pairs[parity][3]
        e = 2 * n + parity
        total = [None] * 4
        for b in range(BASES):
            high = jnp.concatenate([source[0, b, i] for i in range(4)], axis=1)
            low = jnp.concatenate([source[1, b, i] for i in range(4)], axis=1)
            smeared = jnp.dot(
                band[n, b][:, 0 : 3 * ROWS],
                jnp.concatenate([high, low, high], axis=0),
                preferred_element_type=f32,
            )
            for i in range(4):
                k = HALVES[half][i % 2]
                plane = coef[e, b, :, k * LANES : (k + 1) * LANES].astype(f32)
                term = smeared[:, i * LANES : (i + 1) * LANES] * plane
                total[i] = term if total[i] is None else total[i] + term
        for i in range(2):
            weight = 1.0 / (total[2 + i] + READ_NOISE)
            val[half, e, 0, i] = weight * total[i]
            val[half, e, 1, i] = weight

    def smear(half):
        def prepare(parity, n):
            if half == 0:
                build(parity, n)
                extend(parity, n)

        def step(n, _):
            later = (n + 1) % (EPOCHS // 2)
            spread(half, 1, n, col1)
            prepare(0, later)
            finish(half, 0, n, col0)
            spread(half, 0, later, col0)
            prepare(1, later)
            finish(half, 1, n, col1)
            return 0

        prepare(0, 0)
        prepare(1, 0)
        spread(half, 0, 0, col0)
        lax.fori_loop(0, EPOCHS // 2, step, 0)

    def select(half, index, _):
        f, i = index // (2 * SIDE), index // SIDE % 2
        rows = pl.ds(pl.multiple_of(index % SIDE * 8, 8), 8)
        values = [val[half, e, f, i, rows, :] for e in range(EPOCHS)]
        sorts = [sort_four(values[i : i + 4]) for i in range(0, EPOCHS, 4)]
        pairs = []
        for i in (0, 2):
            pairs.append(
                (
                    sort_bitonic(lower_four(sorts[i], sorts[i + 1])),
                    sort_bitonic(upper_four(sorts[i], sorts[i + 1])),
                )
            )
        low, high = merge_ends(pairs[0], pairs[1])
        for place, value in enumerate(low + high + [sum_tree(values)]):
            lists[half, place, index // SIDE, index % SIDE] = value
        return 0

    def copy_to(source, target, send, receive, dy, dx):
        copy = pltpu.make_async_remote_copy(
            src_ref=source,
            dst_ref=target,
            send_sem=send,
            recv_sem=receive,
            device_id=(peer_at(dy, dx), sky),
            device_id_type=MESH,
        )
        copy.start()
        return copy

    def send_near(half):
        copies = []
        for step in (2, 1, 3):
            x, y = (my_x + step) % SIDE, (my_y + step) % SIDE
            sems = [(near_send.at[half, i, step - 1], near_recv.at[half, i, step - 1]) for i in range(2)]
            low = copy_to(
                lists.at[half, pl.ds(0, REJECT), x], near_low.at[half, step - 1], *sems[0], 0, step
            )
            high = copy_to(
                lists.at[half, pl.ds(REJECT, REJECT + 1), :, y],
                near_high.at[half, step - 1],
                *sems[1],
                step,
                0,
            )
            copies += [low, high]
        return copies

    def tree(parts, pick):
        while len(parts) > 1:
            parts = [sort_bitonic(pick(parts[i], parts[i + 1])) for i in range(0, len(parts), 2)]
        return parts[0]

    def send_far(half, copies):
        for copy in copies:
            copy.wait_recv()
        for g in range(SIDE):
            parts = [[lists[half, i, my_x, g] for i in range(REJECT)]]
            for step in range(SIDE - 1):
                parts.append([near_low[half, step, i, g] for i in range(REJECT)])
            for i, value in enumerate(tree(parts, lower_four)):
                mid_low[half, i, g] = value
            parts = [[lists[half, REJECT + i, g, my_y] for i in range(REJECT + 1)]]
            for step in range(SIDE - 1):
                parts.append([near_high[half, step, i, g] for i in range(REJECT + 1)])
            for i, value in enumerate(tree([part[0:REJECT] for part in parts], upper_four)):
                mid_high[half, i, g] = value
            mid_high[half, REJECT, g] = sum_tree([part[REJECT] for part in parts])
        result = []
        for step in (2, 1, 3):
            x, y = (my_x + step) % SIDE, (my_y + step) % SIDE
            sems = [(far_send.at[half, i, step - 1], far_recv.at[half, i, step - 1]) for i in range(2)]
            low = copy_to(mid_low.at[half, :, y], far_low.at[half, step - 1], *sems[0], step, 0)
            high = copy_to(mid_high.at[half, :, x], far_high.at[half, step - 1], *sems[1], 0, step)
            result += [low, high]
        return result

    def close(half, copies):
        for copy in copies:
            copy.wait_recv()
        lows = [[mid_low[half, i, my_y] for i in range(REJECT)]]
        highs = [[mid_high[half, i, my_x] for i in range(REJECT + 1)]]
        for step in range(SIDE - 1):
            lows.append([far_low[half, step, i] for i in range(REJECT)])
            highs.append([far_high[half, step, i] for i in range(REJECT + 1)])
        low = lower_four(*(sort_bitonic(lower_four(lows[i], lows[i + 1])) for i in (0, 2)))
        high = upper_four(*(sort_bitonic(upper_four(highs[i], highs[i + 1])) for i in (0, 2)))
        total = sum_tree([part[REJECT] for part in highs])
        final[me, half] = total - sum_tree(low) - sum_tree(high)

    loads[5].wait()
    smear(0)
    lax.fori_loop(0, PEERS, lambda index, _: select(0, index, _), 0, unroll=2)
    near0 = send_near(0)
    for copy in halo_copies:
        copy.wait_recv()
    for side, at_end in ((0, 0), (1, strips - 1)):
        for f in range(2):
            value = halo[1 - side, f] * jnp.where(sky == at_end, 0.0, 1.0)
            high, low = split(value)
            edge[side, 0, f] = high
            edge[side, 1, f] = low.astype(bf16)
    smear(1)
    lax.fori_loop(0, PEERS, lambda index, _: select(1, index, _), 0, unroll=2)
    near1 = send_near(1)
    far0 = send_far(0, near0)
    far1 = send_far(1, near1)
    close(0, far0)
    close(1, far1)

    copies = [
        copy_to(final.at[me], final.at[me], fin_send.at[i], fin_recv.at[i], dy, dx)
        for i, (dy, dx) in enumerate(offsets)
    ]
    for i, (dy, dx) in enumerate(offsets):
        source = peer_at(SIDE - dy, SIDE - dx)
        pltpu.make_async_remote_copy(
            src_ref=final.at[source],
            dst_ref=final.at[source],
            send_sem=fin_send.at[i],
            recv_sem=fin_recv.at[i],
            device_id=(source, sky),
            device_id_type=MESH,
        ).wait_recv()

    for half, blocks in enumerate(HALVES):
        for unit in range(PEERS):
            f, k, g = unit // (2 * SIDE), blocks[unit // SIDE % 2], unit % SIDE
            out_ref[f, 8 * g : 8 * g + 8, k * LANES : (k + 1) * LANES] = final[
                (unit % SIDE) * SIDE + unit // SIDE, half
            ]

    for copy in halo_copies + near0 + near1 + far0 + far1 + copies:
        copy.wait_send()


def per_device(images, variances, coefficients, row_filters, col_filters, dithers):
    f32, bf16 = jnp.float32, jnp.bfloat16
    dma, vmem = pltpu.SemaphoreType.DMA, pltpu.VMEM
    tile = (OWNER_ROWS, LANES)
    trimmed = pl.pallas_call(
        kernel,
        out_shape=jax.ShapeDtypeStruct((2, ROWS, BLOCKS * LANES), f32),
        in_specs=[pl.BlockSpec(memory_space=pl.ANY)] * 6,
        out_specs=pl.BlockSpec(memory_space=pltpu.VMEM),
        scratch_shapes=[
            vmem((EPOCHS, ROWS, BLOCKS * LANES), f32),
            vmem((EPOCHS, ROWS, BLOCKS * LANES), f32),
            vmem((EPOCHS, BASES, ROWS, BLOCKS * LANES), bf16),
            vmem((TAPS, BASES, EPOCHS), f32),
            vmem((TAPS, BASES, EPOCHS), f32),
            pltpu.SMEM((2, EPOCHS), jnp.int32),
            vmem((LANES, LANES), f32),
            vmem((4, EPOCHS * BASES * 8, LANES), f32),
            *(
                2
                * [
                vmem((EPOCHS // 2, BASES, LANES, LANES), bf16),
                vmem((EPOCHS // 2, BASES, LANES, LANES), bf16),
                vmem((EPOCHS // 2, BASES, 48, LANES), bf16),
                vmem((EPOCHS // 2, BASES, ROWS, LANES), bf16),
                vmem((EPOCHS // 2, 2, BLOCKS, ROWS, LANES), bf16),
                vmem((EPOCHS // 2, 2, BLOCKS, ROWS, LANES), bf16),
                vmem((EPOCHS // 2, 2, BLOCKS, ROWS, LANES), bf16),
                ]
            ),
            vmem((2, 2, ROWS, LANES), f32),
            vmem((2, 2, ROWS, LANES), f32),
            vmem((2, 2, 2, ROWS, LANES), bf16),
            vmem((2, BASES, 4, ROWS, LANES), bf16),
            vmem((2, BASES, 4, ROWS, LANES), bf16),
            vmem((2, EPOCHS, 2, 2, ROWS, LANES), f32),
            vmem((2, LISTS, SIDE, SIDE) + tile, f32),
            vmem((2, SIDE - 1, REJECT, SIDE) + tile, f32),
            vmem((2, SIDE - 1, REJECT + 1, SIDE) + tile, f32),
            vmem((2, REJECT, SIDE) + tile, f32),
            vmem((2, REJECT + 1, SIDE) + tile, f32),
            vmem((2, SIDE - 1, REJECT) + tile, f32),
            vmem((2, SIDE - 1, REJECT + 1) + tile, f32),
            vmem((PEERS, 2) + tile, f32),
            dma((6,)),
            dma((2,)),
            dma((2,)),
            dma((2, 2, SIDE - 1)),
            dma((2, 2, SIDE - 1)),
            dma((2, 2, SIDE - 1)),
            dma((2, 2, SIDE - 1)),
            dma((PEERS - 1,)),
            dma((PEERS - 1,)),
        ],
        compiler_params=pltpu.CompilerParams(
            collective_id=0, has_side_effects=True, vmem_limit_bytes=66_000_000
        ),
        name="coadd",
    )(
        images,
        variances,
        coefficients,
        jnp.transpose(row_filters, (2, 1, 0)),
        jnp.transpose(col_filters, (2, 1, 0)),
        jnp.transpose(dithers),
    )
    kept_count = float(EPOCHS * lax.axis_size("epoch") - 2 * REJECT)
    return trimmed[0] / trimmed[1], trimmed[1] / kept_count


def solution(mesh):
    placed = (
        P("epoch", None, "sky"),
        P("epoch", None, "sky"),
        P("epoch", None, None, "sky"),
        P("epoch", None, None),
        P("epoch", None, None),
        P("epoch", None),
    )
    return jax.shard_map(
        per_device,
        mesh=mesh,
        in_specs=placed,
        out_specs=(P(None, "sky"), P(None, "sky")),
        check_vma=False,
    )
```

```python
import jax
import jax.numpy as jnp
from jax import lax
from jax.experimental import pallas as pl
from jax.experimental.pallas import tpu as pltpu
from jax.sharding import PartitionSpec as P

TAPS = 11
BASES = 4
REJECT = 4
HALF = 5
HALO = 8
READ_NOISE = 0.25

LANES = 128
EPOCHS = 16
ROWS = 32
BLOCKS = 4
SIDE = 4
PEERS = SIDE * SIDE
LISTS = 2 * REJECT + 1
HALVES = ((1, 2), (0, 3))
OWNER_ROWS = 8
MESH = pl.DeviceIdType.MESH


def split(value):
    high = value.astype(jnp.bfloat16)
    return high, value - high.astype(jnp.float32)


def exchange(first, second):
    return jnp.minimum(first, second), jnp.maximum(first, second)


def sort_four(values):
    a, b, c, d = values
    a, b = exchange(a, b)
    c, d = exchange(c, d)
    a, c = exchange(a, c)
    b, d = exchange(b, d)
    b, c = exchange(b, c)
    return [a, b, c, d]


def sort_bitonic(values):
    a, b, c, d = values
    a, c = exchange(a, c)
    b, d = exchange(b, d)
    a, b = exchange(a, b)
    c, d = exchange(c, d)
    return [a, b, c, d]


def lower_four(first, second):
    return [jnp.minimum(first[i], second[REJECT - 1 - i]) for i in range(REJECT)]


def upper_four(first, second):
    return [jnp.maximum(first[i], second[REJECT - 1 - i]) for i in range(REJECT)]


def merge_ends(first, second, last=False):
    low = lower_four(first[0], second[0])
    high = upper_four(first[1], second[1])
    if not last:
        low, high = sort_bitonic(low), sort_bitonic(high)
    return low, high


def sum_tree(values):
    values = list(values)
    while len(values) > 1:
        values = [values[i] + values[i + 1] for i in range(0, len(values) - 1, 2)] + (
            [values[-1]] if len(values) % 2 else []
        )
    return values[0]


def kernel(
    img_hbm, var_hbm, coef_hbm, rowf_hbm, colf_hbm, dith_hbm, out_ref,
    img, var, coef, rowf, colf, dith, filt, base, pack, halo, edge, col0, col1, val, lists,
    near_low, near_high, mid_low, mid_high, far_low, far_high, final,
    in_sem, halo_send, halo_recv, near_send, near_recv, far_send, far_recv, fin_send, fin_recv,
):
    f32, bf16 = jnp.float32, jnp.bfloat16
    me = lax.axis_index("epoch")
    sky = lax.axis_index("sky")
    strips = lax.axis_size("sky")
    my_y, my_x = me // SIDE, me % SIDE
    right, left = (sky + 1) % strips, (sky + strips - 1) % strips

    def peer_at(dy, dx):
        return ((my_y + dy) % SIDE) * SIDE + (my_x + dx) % SIDE

    offsets = [(dy, dx) for dy in (2, 1, 3, 0) for dx in (2, 1, 3, 0) if dy or dx]
    offsets.sort(key=lambda o: -(2 - abs(2 - o[0]) + 2 - abs(2 - o[1])))

    loads = [
        pltpu.make_async_copy(source, target, in_sem.at[i])
        for i, (source, target) in enumerate(
            (
                (rowf_hbm, rowf),
                (colf_hbm, colf),
                (dith_hbm, dith),
                (img_hbm, img),
                (var_hbm, var),
                (coef_hbm, coef),
            )
        )
    ]
    for load in loads:
        load.start()

    barrier = pltpu.get_barrier_semaphore()
    for neighbour in (left, right):
        pl.semaphore_signal(barrier, inc=1, device_id=(me, neighbour), device_id_type=MESH)
    for dy, dx in offsets:
        pl.semaphore_signal(barrier, inc=1, device_id=(peer_at(dy, dx), sky), device_id_type=MESH)

    lane = lax.broadcasted_iota(jnp.int32, (ROWS, LANES), 1)
    lane16 = lane[0:16]

    def within(start, stop, like=lane):
        return jnp.where((like >= start) & (like < stop), 1.0, 0.0).astype(bf16)

    filt[...] = jnp.zeros_like(filt)
    loads[0].wait()
    loads[1].wait()
    for j in range(TAPS):
        for b in range(BASES):
            filt[16 * b + j, 0:EPOCHS] = rowf[j, b, :]
            filt[64 + 16 * b + TAPS - 1 - j, 0:EPOCHS] = colf[j, b, :]
    turned = jnp.transpose(filt[...])[0:EPOCHS]
    for kind in range(2):
        for b in range(BASES):
            at = 16 * (BASES * kind + b)
            taps = pltpu.roll(turned, LANES - at, 1) if at else turned
            taps = jnp.where(lane16 < 16, taps, 0.0)
            high, low = split(taps)
            high, low = high.astype(f32), low.astype(bf16).astype(f32)
            if kind == 0:
                parts = high + pltpu.roll(high, ROWS, 1) + pltpu.roll(low, 2 * ROWS, 1)
            else:
                parts = high + pltpu.roll(low, 64, 1)
            base[kind, b * EPOCHS : (b + 1) * EPOCHS, :] = parts

    loads[3].wait()
    loads[4].wait()
    fields = (img, var)
    last_cols = slice((BLOCKS - 1) * LANES, BLOCKS * LANES)

    def gather_edges(e, _):
        mine = (lane >= HALO * e) & (lane < HALO * (e + 1))
        for f in range(2):
            first = pltpu.roll(fields[f][e, :, 0:LANES], HALO * e, 1)
            last = pltpu.roll(fields[f][e, :, last_cols], (HALO * e + HALO) % LANES, 1)
            pack[0, f] = jnp.where(mine, first, pack[0, f])
            pack[1, f] = jnp.where(mine, last, pack[1, f])
        return 0

    lax.fori_loop(0, EPOCHS, gather_edges, 0, unroll=4)

    loads[2].wait()

    def filters(which, b, e):
        taps = jnp.broadcast_to(base[which, pl.ds(b * EPOCHS + e, 1), :], (16, LANES))
        return pltpu.roll(taps, 0, 1, stride=1, stride_axis=0).astype(bf16)

    near_row = []
    for g in range(2):
        apart = lane16 % ROWS - lax.broadcasted_iota(jnp.int32, (16, LANES), 0) - 16 * g
        near_row.append(jnp.where((apart <= 8) & (apart >= -8), 1.0, 0.0).astype(bf16))

    def band_of(b, e):
        taps = filters(0, b, e)
        groups = [
            pltpu.roll(taps, 8 - dith[0, e] + (16 * g - HALF - 8) % LANES, 1) * near_row[g]
            for g in range(2)
        ]
        return jnp.concatenate(groups, axis=0)[:, 0 : 3 * ROWS]

    def toeplitz_of(b, e):
        taps = filters(1, b, e)
        turned = [
            pltpu.roll(taps, dith[1, e] + (16 * g - HALO - HALF) % LANES, 1) for g in range(8)
        ]
        windows = [within(max(0, 16 * g - 16), 16 * g + 16, lane16) for g in range(8)]
        high = [turned[g] * windows[g] for g in range(8)]
        low = [turned[(g + 4) % 8] * windows[g] for g in range(8)]
        tail_high, tail_low = (turned[g] * within(112, LANES, lane16) for g in (0, 4))
        return jnp.concatenate(high + high + low + [tail_high, tail_high, tail_low], axis=0)

    def spread(half, e, target):
        highs, lows, tails = [], [], []
        for f in range(2):
            cache = {}

            def turned(t):
                if t < 0:
                    return pltpu.roll(edge[0, f], (LANES - HALO * e) % LANES, 1)
                if t == BLOCKS:
                    return pltpu.roll(edge[1, f], (LANES + HALO - HALO * e) % LANES, 1)
                if t not in cache:
                    cache[t] = pltpu.roll(fields[f][e, :, t * LANES : (t + 1) * LANES], HALO, 1)
                return cache[t]

            def tile(t):
                if (t, 0) not in cache:
                    high, low = split(jnp.where(lane < HALO, turned(t - 1), turned(t)))
                    cache[t, 0] = high, low.astype(bf16)
                return cache[t, 0]

            for k in HALVES[half]:
                high, low = tile(k)
                highs.append(high)
                lows.append(low)
                high, low = tile(k + 1)
                tails.append(
                    high * within(0, 16)
                    + pltpu.roll(low, 16, 1) * within(16, 32)
                    + pltpu.roll(high, 32, 1) * within(32, 48)
                )
        highs, lows, tails = (jnp.concatenate(parts, axis=0) for parts in (highs, lows, tails))
        data = jnp.concatenate([highs, lows, highs, tails], axis=1)
        taps = jnp.concatenate([toeplitz_of(b, e) for b in range(BASES)], axis=1)
        result = jnp.dot(data[:, 0 : taps.shape[0]], taps, preferred_element_type=f32)
        high, low = split(result)
        low = low.astype(bf16)
        for b in range(BASES):
            for i in range(4):
                rows, lanes = slice(i * ROWS, (i + 1) * ROWS), slice(b * LANES, (b + 1) * LANES)
                target[0, b, i] = high[rows, lanes]
                target[1, b, i] = low[rows, lanes]

    def finish(half, e, source):
        total = [None] * 4
        for b in range(BASES):
            high = jnp.concatenate([source[0, b, i] for i in range(4)], axis=1)
            low = jnp.concatenate([source[1, b, i] for i in range(4)], axis=1)
            smeared = jnp.dot(
                band_of(b, e),
                jnp.concatenate([high, low, high], axis=0),
                preferred_element_type=f32,
            )
            for i in range(4):
                k = HALVES[half][i % 2]
                plane = coef[e, b, :, k * LANES : (k + 1) * LANES].astype(f32)
                term = smeared[:, i * LANES : (i + 1) * LANES] * plane
                total[i] = term if total[i] is None else total[i] + term
        for i in range(2):
            weight = 1.0 / (total[2 + i] + READ_NOISE)
            val[half, e, 0, i] = weight * total[i]
            val[half, e, 1, i] = weight

    def send_halos():
        pl.semaphore_wait(barrier, 2 + len(offsets))
        halo_copies = []
        for side, target in ((0, left), (1, right)):
            copy = pltpu.make_async_remote_copy(
                src_ref=pack.at[side],
                dst_ref=halo.at[side],
                send_sem=halo_send.at[side],
                recv_sem=halo_recv.at[side],
                device_id=(me, target),
                device_id_type=MESH,
            )
            copy.start()
            halo_copies.append(copy)
        return halo_copies

    def smear(half, start, stop):
        def step(n, _):
            e = 2 * n
            spread(half, e + 1, col1)
            finish(half, e, col0)
            spread(half, (e + 2) % EPOCHS, col0)
            finish(half, e + 1, col1)
            return 0

        if start == 0:
            spread(half, 0, col0)
        lax.fori_loop(start, stop, step, 0)

    def select(half, index, _):
        f, i = index // (2 * SIDE), index // SIDE % 2
        rows = pl.ds(pl.multiple_of(index % SIDE * 8, 8), 8)
        values = [val[half, e, f, i, rows, :] for e in range(EPOCHS)]
        sorts = [sort_four(values[i : i + 4]) for i in range(0, EPOCHS, 4)]
        pairs = []
        for i in (0, 2):
            pairs.append(
                (
                    sort_bitonic(lower_four(sorts[i], sorts[i + 1])),
                    sort_bitonic(upper_four(sorts[i], sorts[i + 1])),
                )
            )
        low, high = merge_ends(pairs[0], pairs[1])
        for place, value in enumerate(low + high + [sum_tree(values)]):
            lists[half, place, index // SIDE, index % SIDE] = value
        return 0

    def copy_to(source, target, send, receive, dy, dx):
        copy = pltpu.make_async_remote_copy(
            src_ref=source,
            dst_ref=target,
            send_sem=send,
            recv_sem=receive,
            device_id=(peer_at(dy, dx), sky),
            device_id_type=MESH,
        )
        copy.start()
        return copy

    def send_near(half):
        copies = []
        for step in (2, 1, 3):
            x, y = (my_x + step) % SIDE, (my_y + step) % SIDE
            sems = [(near_send.at[half, i, step - 1], near_recv.at[half, i, step - 1]) for i in range(2)]
            low = copy_to(
                lists.at[half, pl.ds(0, REJECT), x], near_low.at[half, step - 1], *sems[0], 0, step
            )
            high = copy_to(
                lists.at[half, pl.ds(REJECT, REJECT + 1), :, y],
                near_high.at[half, step - 1],
                *sems[1],
                step,
                0,
            )
            copies += [low, high]
        return copies

    def tree(parts, pick):
        while len(parts) > 1:
            parts = [sort_bitonic(pick(parts[i], parts[i + 1])) for i in range(0, len(parts), 2)]
        return parts[0]

    def send_far(half, copies):
        for copy in copies:
            copy.wait_recv()
        for g in range(SIDE):
            parts = [[lists[half, i, my_x, g] for i in range(REJECT)]]
            for step in range(SIDE - 1):
                parts.append([near_low[half, step, i, g] for i in range(REJECT)])
            for i, value in enumerate(tree(parts, lower_four)):
                mid_low[half, i, g] = value
            parts = [[lists[half, REJECT + i, g, my_y] for i in range(REJECT + 1)]]
            for step in range(SIDE - 1):
                parts.append([near_high[half, step, i, g] for i in range(REJECT + 1)])
            for i, value in enumerate(tree([part[0:REJECT] for part in parts], upper_four)):
                mid_high[half, i, g] = value
            mid_high[half, REJECT, g] = sum_tree([part[REJECT] for part in parts])
        result = []
        for step in (2, 1, 3):
            x, y = (my_x + step) % SIDE, (my_y + step) % SIDE
            sems = [(far_send.at[half, i, step - 1], far_recv.at[half, i, step - 1]) for i in range(2)]
            low = copy_to(mid_low.at[half, :, y], far_low.at[half, step - 1], *sems[0], step, 0)
            high = copy_to(mid_high.at[half, :, x], far_high.at[half, step - 1], *sems[1], 0, step)
            result += [low, high]
        return result

    def close(half, copies):
        for copy in copies:
            copy.wait_recv()
        lows = [[mid_low[half, i, my_y] for i in range(REJECT)]]
        highs = [[mid_high[half, i, my_x] for i in range(REJECT + 1)]]
        for step in range(SIDE - 1):
            lows.append([far_low[half, step, i] for i in range(REJECT)])
            highs.append([far_high[half, step, i] for i in range(REJECT + 1)])
        low = lower_four(*(sort_bitonic(lower_four(lows[i], lows[i + 1])) for i in (0, 2)))
        high = upper_four(*(sort_bitonic(upper_four(highs[i], highs[i + 1])) for i in (0, 2)))
        total = sum_tree([part[REJECT] for part in highs])
        final[me, half] = total - sum_tree(low) - sum_tree(high)

    loads[5].wait()
    smear(0, 0, 2)
    halo_copies = send_halos()
    smear(0, 2, EPOCHS // 2)
    lax.fori_loop(0, PEERS, lambda index, _: select(0, index, _), 0, unroll=2)
    near0 = send_near(0)
    for copy in halo_copies:
        copy.wait_recv()
    for side, at_end in ((0, 0), (1, strips - 1)):
        for f in range(2):
            edge[side, f] = halo[1 - side, f] * jnp.where(sky == at_end, 0.0, 1.0)
    smear(1, 0, EPOCHS // 2)
    lax.fori_loop(0, PEERS, lambda index, _: select(1, index, _), 0, unroll=2)
    near1 = send_near(1)
    far0 = send_far(0, near0)
    far1 = send_far(1, near1)
    close(0, far0)
    close(1, far1)

    copies = [
        copy_to(final.at[me], final.at[me], fin_send.at[i], fin_recv.at[i], dy, dx)
        for i, (dy, dx) in enumerate(offsets)
    ]
    for i, (dy, dx) in enumerate(offsets):
        source = peer_at(SIDE - dy, SIDE - dx)
        pltpu.make_async_remote_copy(
            src_ref=final.at[source],
            dst_ref=final.at[source],
            send_sem=fin_send.at[i],
            recv_sem=fin_recv.at[i],
            device_id=(source, sky),
            device_id_type=MESH,
        ).wait_recv()

    for half, blocks in enumerate(HALVES):
        for unit in range(PEERS):
            f, k, g = unit // (2 * SIDE), blocks[unit // SIDE % 2], unit % SIDE
            out_ref[f, 8 * g : 8 * g + 8, k * LANES : (k + 1) * LANES] = final[
                (unit % SIDE) * SIDE + unit // SIDE, half
            ]

    for copy in halo_copies + near0 + near1 + far0 + far1 + copies:
        copy.wait_send()


def per_device(images, variances, coefficients, row_filters, col_filters, dithers):
    f32, bf16 = jnp.float32, jnp.bfloat16
    dma, vmem = pltpu.SemaphoreType.DMA, pltpu.VMEM
    tile = (OWNER_ROWS, LANES)
    trimmed = pl.pallas_call(
        kernel,
        out_shape=jax.ShapeDtypeStruct((2, ROWS, BLOCKS * LANES), f32),
        in_specs=[pl.BlockSpec(memory_space=pltpu.HBM)] * 6,
        out_specs=pl.BlockSpec(memory_space=pltpu.VMEM),
        scratch_shapes=[
            vmem((EPOCHS, ROWS, BLOCKS * LANES), f32),
            vmem((EPOCHS, ROWS, BLOCKS * LANES), f32),
            vmem((EPOCHS, BASES, ROWS, BLOCKS * LANES), bf16),
            vmem((TAPS, BASES, EPOCHS), f32),
            vmem((TAPS, BASES, EPOCHS), f32),
            pltpu.SMEM((2, EPOCHS), jnp.int32),
            vmem((LANES, LANES), f32),
            vmem((2, EPOCHS * BASES, LANES), f32),
            vmem((2, 2, ROWS, LANES), f32),
            vmem((2, 2, ROWS, LANES), f32),
            vmem((2, 2, ROWS, LANES), f32),
            vmem((2, BASES, 4, ROWS, LANES), bf16),
            vmem((2, BASES, 4, ROWS, LANES), bf16),
            vmem((2, EPOCHS, 2, 2, ROWS, LANES), f32),
            vmem((2, LISTS, SIDE, SIDE) + tile, f32),
            vmem((2, SIDE - 1, REJECT, SIDE) + tile, f32),
            vmem((2, SIDE - 1, REJECT + 1, SIDE) + tile, f32),
            vmem((2, REJECT, SIDE) + tile, f32),
            vmem((2, REJECT + 1, SIDE) + tile, f32),
            vmem((2, SIDE - 1, REJECT) + tile, f32),
            vmem((2, SIDE - 1, REJECT + 1) + tile, f32),
            vmem((PEERS, 2) + tile, f32),
            dma((6,)),
            dma((2,)),
            dma((2,)),
            dma((2, 2, SIDE - 1)),
            dma((2, 2, SIDE - 1)),
            dma((2, 2, SIDE - 1)),
            dma((2, 2, SIDE - 1)),
            dma((PEERS - 1,)),
            dma((PEERS - 1,)),
        ],
        compiler_params=pltpu.CompilerParams(
            collective_id=0, has_side_effects=True, vmem_limit_bytes=66_000_000
        ),
        name="coadd",
    )(
        images,
        variances,
        coefficients,
        jnp.transpose(row_filters, (2, 1, 0)),
        jnp.transpose(col_filters, (2, 1, 0)),
        jnp.transpose(dithers),
    )
    kept_count = float(EPOCHS * lax.axis_size("epoch") - 2 * REJECT)
    return trimmed[0] / trimmed[1], trimmed[1] / kept_count


def solution(mesh):
    placed = (
        P("epoch", None, "sky"),
        P("epoch", None, "sky"),
        P("epoch", None, None, "sky"),
        P("epoch", None, None),
        P("epoch", None, None),
        P("epoch", None),
    )
    return jax.shard_map(
        per_device,
        mesh=mesh,
        in_specs=placed,
        out_specs=(P(None, "sky"), P(None, "sky")),
        check_vma=False,
    )
```

```python
import jax
import jax.numpy as jnp
from jax import lax
from jax.experimental import pallas as pl
from jax.experimental.pallas import tpu as pltpu
from jax.sharding import PartitionSpec as P

TAPS = 11
BASES = 4
REJECT = 4
HALF = 5
HALO = 8
READ_NOISE = 0.25

LANES = 128
EPOCHS = 16
FIRST = 6
ROWS = 32
BLOCKS = 4
SIDE = 4
PEERS = SIDE * SIDE
LISTS = 2 * REJECT + 1
HALVES = ((1, 2), (0, 3))
OWNER_ROWS = 8
MESH = pl.DeviceIdType.MESH


def split(value):
    high = value.astype(jnp.bfloat16)
    return high, value - high.astype(jnp.float32)


def exchange(first, second):
    return jnp.minimum(first, second), jnp.maximum(first, second)


def sort_four(values):
    a, b, c, d = values
    a, b = exchange(a, b)
    c, d = exchange(c, d)
    a, c = exchange(a, c)
    b, d = exchange(b, d)
    b, c = exchange(b, c)
    return [a, b, c, d]


def sort_bitonic(values):
    a, b, c, d = values
    a, c = exchange(a, c)
    b, d = exchange(b, d)
    a, b = exchange(a, b)
    c, d = exchange(c, d)
    return [a, b, c, d]


def lower_four(first, second):
    return [jnp.minimum(first[i], second[REJECT - 1 - i]) for i in range(REJECT)]


def upper_four(first, second):
    return [jnp.maximum(first[i], second[REJECT - 1 - i]) for i in range(REJECT)]


def merge_ends(first, second, last=False):
    low = lower_four(first[0], second[0])
    high = upper_four(first[1], second[1])
    if not last:
        low, high = sort_bitonic(low), sort_bitonic(high)
    return low, high


def sum_tree(values):
    values = list(values)
    while len(values) > 1:
        values = [values[i] + values[i + 1] for i in range(0, len(values) - 1, 2)] + (
            [values[-1]] if len(values) % 2 else []
        )
    return values[0]


def kernel(
    img_hbm, var_hbm, coef_hbm, rowf_hbm, colf_hbm, dith_hbm, out_ref,
    img, var, coef, rowf, colf, dith, filt, base, pack, halo, edge, col0, col1, col2, col3, val, lists,
    near_low, near_high, mid_low, mid_high, far_low, far_high, final,
    in_sem, halo_send, halo_recv, near_send, near_recv, far_send, far_recv, fin_send, fin_recv,
):
    f32, bf16 = jnp.float32, jnp.bfloat16
    me = lax.axis_index("epoch")
    sky = lax.axis_index("sky")
    strips = lax.axis_size("sky")
    my_y, my_x = me // SIDE, me % SIDE
    right, left = (sky + 1) % strips, (sky + strips - 1) % strips

    def peer_at(dy, dx):
        return ((my_y + dy) % SIDE) * SIDE + (my_x + dx) % SIDE

    offsets = [(dy, dx) for dy in (2, 1, 3, 0) for dx in (2, 1, 3, 0) if dy or dx]
    offsets.sort(key=lambda o: -(2 - abs(2 - o[0]) + 2 - abs(2 - o[1])))

    loads = [
        pltpu.make_async_copy(source, target, in_sem.at[i])
        for i, (source, target) in enumerate(((rowf_hbm, rowf), (colf_hbm, colf), (dith_hbm, dith)))
    ]
    portions = []
    for start, count in ((0, FIRST), (FIRST, EPOCHS - FIRST)):
        rows, part = pl.ds(start, count), []
        for source, target in ((img_hbm, img), (var_hbm, var), (coef_hbm, coef)):
            sem = in_sem.at[3 + 3 * len(portions) + len(part)]
            part.append(pltpu.make_async_copy(source.at[rows], target.at[rows], sem))
        portions.append(part)
    for load in loads + portions[0] + portions[1]:
        load.start()

    barrier = pltpu.get_barrier_semaphore()
    for neighbour in (left, right):
        pl.semaphore_signal(barrier, inc=1, device_id=(me, neighbour), device_id_type=MESH)
    for dy, dx in offsets:
        pl.semaphore_signal(barrier, inc=1, device_id=(peer_at(dy, dx), sky), device_id_type=MESH)

    lane = lax.broadcasted_iota(jnp.int32, (ROWS, LANES), 1)
    lane16 = lane[0:16]

    def within(start, stop, like=lane):
        return jnp.where((like >= start) & (like < stop), 1.0, 0.0).astype(bf16)

    filt[...] = jnp.zeros_like(filt)
    loads[0].wait()
    loads[1].wait()
    for j in range(TAPS):
        for b in range(BASES):
            filt[16 * b + j, 0:EPOCHS] = rowf[j, b, :]
            filt[64 + 16 * b + TAPS - 1 - j, 0:EPOCHS] = colf[j, b, :]
    turned = jnp.transpose(filt[...])[0:EPOCHS]
    for kind in range(2):
        for b in range(BASES):
            at = 16 * (BASES * kind + b)
            taps = pltpu.roll(turned, LANES - at, 1) if at else turned
            taps = jnp.where(lane16 < 16, taps, 0.0)
            high, low = split(taps)
            high, low = high.astype(f32), low.astype(bf16).astype(f32)
            if kind == 0:
                parts = high + pltpu.roll(high, ROWS, 1) + pltpu.roll(low, 2 * ROWS, 1)
            else:
                parts = high + pltpu.roll(low, 64, 1)
            base[kind, b * EPOCHS : (b + 1) * EPOCHS, :] = parts

    fields = (img, var)
    last_cols = slice((BLOCKS - 1) * LANES, BLOCKS * LANES)

    def gather_edges(e, _):
        mine = (lane >= HALO * e) & (lane < HALO * (e + 1))
        for f in range(2):
            first = pltpu.roll(fields[f][e, :, 0:LANES], HALO * e, 1)
            last = pltpu.roll(fields[f][e, :, last_cols], (HALO * e + HALO) % LANES, 1)
            pack[0, f] = jnp.where(mine, first, pack[0, f])
            pack[1, f] = jnp.where(mine, last, pack[1, f])
        return 0

    loads[2].wait()

    def filters(which, b, e):
        taps = jnp.broadcast_to(base[which, pl.ds(b * EPOCHS + e, 1), :], (16, LANES))
        return pltpu.roll(taps, 0, 1, stride=1, stride_axis=0).astype(bf16)

    near_row = []
    for g in range(2):
        apart = lane16 % ROWS - lax.broadcasted_iota(jnp.int32, (16, LANES), 0) - 16 * g
        near_row.append(jnp.where((apart <= 8) & (apart >= -8), 1.0, 0.0).astype(bf16))

    def band_of(b, e):
        taps = filters(0, b, e)
        groups = [
            pltpu.roll(taps, 8 - dith[0, e] + (16 * g - HALF - 8) % LANES, 1) * near_row[g]
            for g in range(2)
        ]
        return jnp.concatenate(groups, axis=0)[:, 0 : 3 * ROWS]

    row16 = lax.broadcasted_iota(jnp.int32, (16, LANES), 0)
    before = jnp.where((row16 >= 8) & (lane16 < 8), 1.0, 0.0).astype(bf16)
    after = jnp.where((row16 < 8) & (lane16 >= LANES - 8), 1.0, 0.0).astype(bf16)

    def toeplitz_of(b, e):
        taps = filters(1, b, e)
        turned = [pltpu.roll(taps, dith[1, e] + (16 * g - HALF) % LANES, 1) for g in range(8)]
        windows = [within(max(0, 16 * g - 8), 16 * g + 24, lane16) for g in range(8)]
        high = [turned[g] * windows[g] for g in range(8)]
        low = [turned[(g + 4) % 8] * windows[g] for g in range(8)]
        before_high, before_low = turned[7] * before, turned[3] * before
        after_high, after_low = turned[0] * after, turned[4] * after
        sides = [before_high, after_high + before_high, after_high + before_low, after_low]
        return jnp.concatenate(high + high + low + sides, axis=0)

    def spread(half, e, target):
        highs, lows, tails = [], [], []
        for f in range(2):

            def tile(t):
                if t < 0:
                    return pltpu.roll(edge[0, f], (2 * LANES - HALO - HALO * e) % LANES, 1)
                if t == BLOCKS:
                    return pltpu.roll(edge[1, f], (LANES - HALO * e) % LANES, 1)
                return fields[f][e, :, t * LANES : (t + 1) * LANES]

            for k in HALVES[half]:
                high, low = split(tile(k))
                highs.append(high)
                lows.append(low.astype(bf16))
                high, low = split(jnp.where(lane < HALO, tile(k + 1), tile(k - 1)))
                tails.append(
                    pltpu.roll(high, 16, 1) * within(8, 24)
                    + pltpu.roll(low.astype(bf16), 32, 1) * within(24, 40)
                    + pltpu.roll(high, 48, 1) * within(40, 56)
                )
        highs, lows, tails = (jnp.concatenate(parts, axis=0) for parts in (highs, lows, tails))
        data = jnp.concatenate([highs, lows, highs, tails], axis=1)
        taps = jnp.concatenate([toeplitz_of(b, e) for b in range(BASES)], axis=1)
        result = jnp.dot(data[:, 0 : taps.shape[0]], taps, preferred_element_type=f32)
        high, low = split(result)
        low = low.astype(bf16)
        for b in range(BASES):
            for i in range(4):
                rows, lanes = slice(i * ROWS, (i + 1) * ROWS), slice(b * LANES, (b + 1) * LANES)
                target[0, b, i] = high[rows, lanes]
                target[1, b, i] = low[rows, lanes]

    def finish(half, e, source):
        total = [None] * 4
        for b in range(BASES):
            high = jnp.concatenate([source[0, b, i] for i in range(4)], axis=1)
            low = jnp.concatenate([source[1, b, i] for i in range(4)], axis=1)
            smeared = jnp.dot(
                band_of(b, e),
                jnp.concatenate([high, low, high], axis=0),
                preferred_element_type=f32,
            )
            for i in range(4):
                k = HALVES[half][i % 2]
                plane = coef[e, b, :, k * LANES : (k + 1) * LANES].astype(f32)
                term = smeared[:, i * LANES : (i + 1) * LANES] * plane
                total[i] = term if total[i] is None else total[i] + term
        for i in range(2):
            weight = 1.0 / (total[2 + i] + READ_NOISE)
            val[half, e, 0, i] = weight * total[i]
            val[half, e, 1, i] = weight

    def send_halos():
        lax.fori_loop(0, EPOCHS, gather_edges, 0, unroll=4)
        pl.semaphore_wait(barrier, 2 + len(offsets))
        halo_copies = []
        for side, target in ((0, left), (1, right)):
            copy = pltpu.make_async_remote_copy(
                src_ref=pack.at[side],
                dst_ref=halo.at[side],
                send_sem=halo_send.at[side],
                recv_sem=halo_recv.at[side],
                device_id=(me, target),
                device_id_type=MESH,
            )
            copy.start()
            halo_copies.append(copy)
        return halo_copies

    def smear(half, start, stop):
        def step(n, _):
            e = 4 * n
            spread(half, e + 2, col2)
            finish(half, e, col0)
            spread(half, e + 3, col3)
            finish(half, e + 1, col1)
            spread(half, (e + 4) % EPOCHS, col0)
            finish(half, e + 2, col2)
            spread(half, (e + 5) % EPOCHS, col1)
            finish(half, e + 3, col3)
            return 0

        if start == 0:
            spread(half, 0, col0)
            spread(half, 1, col1)
        lax.fori_loop(start, stop, step, 0)

    def select(half, index, _):
        f, i = index // (2 * SIDE), index // SIDE % 2
        rows = pl.ds(pl.multiple_of(index % SIDE * 8, 8), 8)
        values = [val[half, e, f, i, rows, :] for e in range(EPOCHS)]
        sorts = [sort_four(values[i : i + 4]) for i in range(0, EPOCHS, 4)]
        pairs = []
        for i in (0, 2):
            pairs.append(
                (
                    sort_bitonic(lower_four(sorts[i], sorts[i + 1])),
                    sort_bitonic(upper_four(sorts[i], sorts[i + 1])),
                )
            )
        low, high = merge_ends(pairs[0], pairs[1])
        for place, value in enumerate(low + high + [sum_tree(values)]):
            lists[half, place, index // SIDE, index % SIDE] = value
        return 0

    def copy_to(source, target, send, receive, dy, dx):
        copy = pltpu.make_async_remote_copy(
            src_ref=source,
            dst_ref=target,
            send_sem=send,
            recv_sem=receive,
            device_id=(peer_at(dy, dx), sky),
            device_id_type=MESH,
        )
        copy.start()
        return copy

    def send_near(half):
        copies = []
        for step in (2, 1, 3):
            x, y = (my_x + step) % SIDE, (my_y + step) % SIDE
            sems = [(near_send.at[half, i, step - 1], near_recv.at[half, i, step - 1]) for i in range(2)]
            low = copy_to(
                lists.at[half, pl.ds(0, REJECT), x], near_low.at[half, step - 1], *sems[0], 0, step
            )
            high = copy_to(
                lists.at[half, pl.ds(REJECT, REJECT + 1), :, y],
                near_high.at[half, step - 1],
                *sems[1],
                step,
                0,
            )
            copies += [low, high]
        return copies

    def tree(parts, pick):
        while len(parts) > 1:
            parts = [sort_bitonic(pick(parts[i], parts[i + 1])) for i in range(0, len(parts), 2)]
        return parts[0]

    def send_far(half, copies):
        for copy in copies:
            copy.wait_recv()
        for g in range(SIDE):
            parts = [[lists[half, i, my_x, g] for i in range(REJECT)]]
            for step in range(SIDE - 1):
                parts.append([near_low[half, step, i, g] for i in range(REJECT)])
            for i, value in enumerate(tree(parts, lower_four)):
                mid_low[half, i, g] = value
            parts = [[lists[half, REJECT + i, g, my_y] for i in range(REJECT + 1)]]
            for step in range(SIDE - 1):
                parts.append([near_high[half, step, i, g] for i in range(REJECT + 1)])
            for i, value in enumerate(tree([part[0:REJECT] for part in parts], upper_four)):
                mid_high[half, i, g] = value
            mid_high[half, REJECT, g] = sum_tree([part[REJECT] for part in parts])
        result = []
        for step in (2, 1, 3):
            x, y = (my_x + step) % SIDE, (my_y + step) % SIDE
            sems = [(far_send.at[half, i, step - 1], far_recv.at[half, i, step - 1]) for i in range(2)]
            low = copy_to(mid_low.at[half, :, y], far_low.at[half, step - 1], *sems[0], step, 0)
            high = copy_to(mid_high.at[half, :, x], far_high.at[half, step - 1], *sems[1], 0, step)
            result += [low, high]
        return result

    def close(half, copies):
        for copy in copies:
            copy.wait_recv()
        lows = [[mid_low[half, i, my_y] for i in range(REJECT)]]
        highs = [[mid_high[half, i, my_x] for i in range(REJECT + 1)]]
        for step in range(SIDE - 1):
            lows.append([far_low[half, step, i] for i in range(REJECT)])
            highs.append([far_high[half, step, i] for i in range(REJECT + 1)])
        low = lower_four(*(sort_bitonic(lower_four(lows[i], lows[i + 1])) for i in (0, 2)))
        high = upper_four(*(sort_bitonic(upper_four(highs[i], highs[i + 1])) for i in (0, 2)))
        total = sum_tree([part[REJECT] for part in highs])
        final[me, half] = total - sum_tree(low) - sum_tree(high)

    for load in portions[0]:
        load.wait()
    smear(0, 0, 1)
    for load in portions[1]:
        load.wait()
    halo_copies = send_halos()
    smear(0, 1, EPOCHS // 4)
    lax.fori_loop(0, PEERS, lambda index, _: select(0, index, _), 0, unroll=2)
    near0 = send_near(0)
    for copy in halo_copies:
        copy.wait_recv()
    for side, at_end in ((0, 0), (1, strips - 1)):
        for f in range(2):
            edge[side, f] = halo[1 - side, f] * jnp.where(sky == at_end, 0.0, 1.0)
    smear(1, 0, EPOCHS // 4)
    lax.fori_loop(0, PEERS, lambda index, _: select(1, index, _), 0, unroll=2)
    near1 = send_near(1)
    far0 = send_far(0, near0)
    far1 = send_far(1, near1)
    close(0, far0)
    close(1, far1)

    copies = [
        copy_to(final.at[me], final.at[me], fin_send.at[i], fin_recv.at[i], dy, dx)
        for i, (dy, dx) in enumerate(offsets)
    ]
    for i, (dy, dx) in enumerate(offsets):
        source = peer_at(SIDE - dy, SIDE - dx)
        pltpu.make_async_remote_copy(
            src_ref=final.at[source],
            dst_ref=final.at[source],
            send_sem=fin_send.at[i],
            recv_sem=fin_recv.at[i],
            device_id=(source, sky),
            device_id_type=MESH,
        ).wait_recv()

    for half, blocks in enumerate(HALVES):
        for unit in range(PEERS):
            f, k, g = unit // (2 * SIDE), blocks[unit // SIDE % 2], unit % SIDE
            out_ref[f, 8 * g : 8 * g + 8, k * LANES : (k + 1) * LANES] = final[
                (unit % SIDE) * SIDE + unit // SIDE, half
            ]

    for copy in halo_copies + near0 + near1 + far0 + far1 + copies:
        copy.wait_send()


def per_device(images, variances, coefficients, row_filters, col_filters, dithers):
    f32, bf16 = jnp.float32, jnp.bfloat16
    dma, vmem = pltpu.SemaphoreType.DMA, pltpu.VMEM
    tile = (OWNER_ROWS, LANES)
    trimmed = pl.pallas_call(
        kernel,
        out_shape=jax.ShapeDtypeStruct((2, ROWS, BLOCKS * LANES), f32),
        in_specs=[pl.BlockSpec(memory_space=pltpu.HBM)] * 6,
        out_specs=pl.BlockSpec(memory_space=pltpu.VMEM),
        scratch_shapes=[
            vmem((EPOCHS, ROWS, BLOCKS * LANES), f32),
            vmem((EPOCHS, ROWS, BLOCKS * LANES), f32),
            vmem((EPOCHS, BASES, ROWS, BLOCKS * LANES), bf16),
            vmem((TAPS, BASES, EPOCHS), f32),
            vmem((TAPS, BASES, EPOCHS), f32),
            pltpu.SMEM((2, EPOCHS), jnp.int32),
            vmem((LANES, LANES), f32),
            vmem((2, EPOCHS * BASES, LANES), f32),
            vmem((2, 2, ROWS, LANES), f32),
            vmem((2, 2, ROWS, LANES), f32),
            vmem((2, 2, ROWS, LANES), f32),
            vmem((2, BASES, 4, ROWS, LANES), bf16),
            vmem((2, BASES, 4, ROWS, LANES), bf16),
            vmem((2, BASES, 4, ROWS, LANES), bf16),
            vmem((2, BASES, 4, ROWS, LANES), bf16),
            vmem((2, EPOCHS, 2, 2, ROWS, LANES), f32),
            vmem((2, LISTS, SIDE, SIDE) + tile, f32),
            vmem((2, SIDE - 1, REJECT, SIDE) + tile, f32),
            vmem((2, SIDE - 1, REJECT + 1, SIDE) + tile, f32),
            vmem((2, REJECT, SIDE) + tile, f32),
            vmem((2, REJECT + 1, SIDE) + tile, f32),
            vmem((2, SIDE - 1, REJECT) + tile, f32),
            vmem((2, SIDE - 1, REJECT + 1) + tile, f32),
            vmem((PEERS, 2) + tile, f32),
            dma((9,)),
            dma((2,)),
            dma((2,)),
            dma((2, 2, SIDE - 1)),
            dma((2, 2, SIDE - 1)),
            dma((2, 2, SIDE - 1)),
            dma((2, 2, SIDE - 1)),
            dma((PEERS - 1,)),
            dma((PEERS - 1,)),
        ],
        compiler_params=pltpu.CompilerParams(
            collective_id=0, has_side_effects=True, vmem_limit_bytes=66_000_000
        ),
        name="coadd",
    )(
        images,
        variances,
        coefficients,
        jnp.transpose(row_filters, (2, 1, 0)),
        jnp.transpose(col_filters, (2, 1, 0)),
        jnp.transpose(dithers),
    )
    kept_count = float(EPOCHS * lax.axis_size("epoch") - 2 * REJECT)
    return trimmed[0] / trimmed[1], trimmed[1] / kept_count


def solution(mesh):
    placed = (
        P("epoch", None, "sky"),
        P("epoch", None, "sky"),
        P("epoch", None, None, "sky"),
        P("epoch", None, None),
        P("epoch", None, None),
        P("epoch", None),
    )
    return jax.shard_map(
        per_device,
        mesh=mesh,
        in_specs=placed,
        out_specs=(P(None, "sky"), P(None, "sky")),
        check_vma=False,
    )
```

```python
import jax
import jax.numpy as jnp
from jax import lax
from jax.experimental import pallas as pl
from jax.experimental.pallas import tpu as pltpu
from jax.sharding import PartitionSpec as P

TAPS = 11
BASES = 4
REJECT = 4
HALF = 5
HALO = 8
READ_NOISE = 0.25

LANES = 128
EPOCHS = 16
FIRST = 6
STEPS = EPOCHS // 4
ROWS = 32
BLOCKS = 4
SIDE = 4
PEERS = SIDE * SIDE
LISTS = 2 * REJECT + 1
HALVES = ((1, 2), (0, 3))
OWNER_ROWS = 8
MESH = pl.DeviceIdType.MESH


def split(value):
    high = value.astype(jnp.bfloat16)
    return high, value - high.astype(jnp.float32)


def exchange(first, second):
    return jnp.minimum(first, second), jnp.maximum(first, second)


def sort_four(values):
    a, b, c, d = values
    a, b = exchange(a, b)
    c, d = exchange(c, d)
    a, c = exchange(a, c)
    b, d = exchange(b, d)
    b, c = exchange(b, c)
    return [a, b, c, d]


def sort_bitonic(values):
    a, b, c, d = values
    a, c = exchange(a, c)
    b, d = exchange(b, d)
    a, b = exchange(a, b)
    c, d = exchange(c, d)
    return [a, b, c, d]


def lower_four(first, second):
    return [jnp.minimum(first[i], second[REJECT - 1 - i]) for i in range(REJECT)]


def upper_four(first, second):
    return [jnp.maximum(first[i], second[REJECT - 1 - i]) for i in range(REJECT)]


def merge_ends(first, second, last=False):
    low = lower_four(first[0], second[0])
    high = upper_four(first[1], second[1])
    if not last:
        low, high = sort_bitonic(low), sort_bitonic(high)
    return low, high


def sum_tree(values):
    values = list(values)
    while len(values) > 1:
        values = [values[i] + values[i + 1] for i in range(0, len(values) - 1, 2)] + (
            [values[-1]] if len(values) % 2 else []
        )
    return values[0]


def kernel(
    img_hbm, var_hbm, coef_hbm, rowf_hbm, colf_hbm, dith_hbm, out_ref,
    img, var, coef, rowf, colf, dith, filt, base, pack, halo, edge, col0, col1, col2, col3, val, lists,
    near_low, near_high, mid_low, mid_high, far_low, far_high, direct, final,
    in_sem, halo_send, halo_recv, near_send, near_recv, far_send, far_recv, dir_send, dir_recv, fin_send, fin_recv,
):
    f32, bf16 = jnp.float32, jnp.bfloat16
    me = lax.axis_index("epoch")
    sky = lax.axis_index("sky")
    strips = lax.axis_size("sky")
    my_y, my_x = me // SIDE, me % SIDE
    right, left = (sky + 1) % strips, (sky + strips - 1) % strips

    def peer_at(dy, dx):
        return ((my_y + dy) % SIDE) * SIDE + (my_x + dx) % SIDE

    offsets = [(dy, dx) for dy in (2, 1, 3, 0) for dx in (2, 1, 3, 0) if dy or dx]
    offsets.sort(key=lambda o: -(2 - abs(2 - o[0]) + 2 - abs(2 - o[1])))

    loads = [
        pltpu.make_async_copy(source, target, in_sem.at[i])
        for i, (source, target) in enumerate(((rowf_hbm, rowf), (colf_hbm, colf), (dith_hbm, dith)))
    ]
    portions = []
    for start, count in ((0, FIRST), (FIRST, EPOCHS - FIRST)):
        rows, part = pl.ds(start, count), []
        for source, target in ((img_hbm, img), (var_hbm, var), (coef_hbm, coef)):
            sem = in_sem.at[3 + 3 * len(portions) + len(part)]
            part.append(pltpu.make_async_copy(source.at[rows], target.at[rows], sem))
        portions.append(part)
    for load in loads + portions[0] + portions[1]:
        load.start()

    barrier = pltpu.get_barrier_semaphore()
    for neighbour in (left, right):
        pl.semaphore_signal(barrier, inc=1, device_id=(me, neighbour), device_id_type=MESH)
    for dy, dx in offsets:
        pl.semaphore_signal(barrier, inc=1, device_id=(peer_at(dy, dx), sky), device_id_type=MESH)

    lane = lax.broadcasted_iota(jnp.int32, (ROWS, LANES), 1)
    lane16 = lane[0:16]

    def within(start, stop, like=lane):
        return jnp.where((like >= start) & (like < stop), 1.0, 0.0).astype(bf16)

    filt[...] = jnp.zeros_like(filt)
    loads[0].wait()
    loads[1].wait()
    for j in range(TAPS):
        for b in range(BASES):
            filt[16 * b + j, 0:EPOCHS] = rowf[j, b, :]
            filt[64 + 16 * b + TAPS - 1 - j, 0:EPOCHS] = colf[j, b, :]
    turned = jnp.transpose(filt[...])[0:EPOCHS]
    for kind in range(2):
        for b in range(BASES):
            at = 16 * (BASES * kind + b)
            taps = pltpu.roll(turned, LANES - at, 1) if at else turned
            taps = jnp.where(lane16 < 16, taps, 0.0)
            high, low = split(taps)
            high, low = high.astype(f32), low.astype(bf16).astype(f32)
            if kind == 0:
                parts = high + pltpu.roll(high, ROWS, 1) + pltpu.roll(low, 2 * ROWS, 1)
            else:
                parts = high + pltpu.roll(low, 64, 1)
            base[kind, b * EPOCHS : (b + 1) * EPOCHS, :] = parts

    fields = (img, var)
    last_cols = slice((BLOCKS - 1) * LANES, BLOCKS * LANES)

    def gather_edges(e, _):
        mine = (lane >= HALO * e) & (lane < HALO * (e + 1))
        for f in range(2):
            first = pltpu.roll(fields[f][e, :, 0:LANES], HALO * e, 1)
            last = pltpu.roll(fields[f][e, :, last_cols], (HALO * e + HALO) % LANES, 1)
            pack[0, f] = jnp.where(mine, first, pack[0, f])
            pack[1, f] = jnp.where(mine, last, pack[1, f])
        return 0

    loads[2].wait()

    def filters(which, b, e):
        taps = jnp.broadcast_to(base[which, pl.ds(b * EPOCHS + e, 1), :], (16, LANES))
        return pltpu.roll(taps, 0, 1, stride=1, stride_axis=0).astype(bf16)

    near_row = []
    for g in range(2):
        apart = lane16 % ROWS - lax.broadcasted_iota(jnp.int32, (16, LANES), 0) - 16 * g
        near_row.append(jnp.where((apart <= 8) & (apart >= -8), 1.0, 0.0).astype(bf16))

    def band_of(b, e):
        taps = filters(0, b, e)
        groups = [
            pltpu.roll(taps, 8 - dith[0, e] + (16 * g - HALF - 8) % LANES, 1) * near_row[g]
            for g in range(2)
        ]
        return jnp.concatenate(groups, axis=0)[:, 0 : 3 * ROWS]

    row16 = lax.broadcasted_iota(jnp.int32, (16, LANES), 0)
    before = jnp.where((row16 >= 8) & (lane16 < 8), 1.0, 0.0).astype(bf16)
    after = jnp.where((row16 < 8) & (lane16 >= LANES - 8), 1.0, 0.0).astype(bf16)

    def toeplitz_of(b, e):
        taps = filters(1, b, e)
        turned = [pltpu.roll(taps, dith[1, e] + (16 * g - HALF) % LANES, 1) for g in range(8)]
        windows = [within(max(0, 16 * g - 8), 16 * g + 24, lane16) for g in range(8)]
        high = [turned[g] * windows[g] for g in range(8)]
        low = [turned[(g + 4) % 8] * windows[g] for g in range(8)]
        before_high, before_low = turned[7] * before, turned[3] * before
        after_high, after_low = turned[0] * after, turned[4] * after
        sides = [before_high, after_high + before_high, after_high + before_low, after_low]
        return jnp.concatenate(high + high + low + sides, axis=0)

    def spread(half, e, target):
        highs, lows, tails = [], [], []
        for f in range(2):

            def tile(t):
                if t < 0:
                    return pltpu.roll(edge[0, f], (2 * LANES - HALO - HALO * e) % LANES, 1)
                if t == BLOCKS:
                    return pltpu.roll(edge[1, f], (LANES - HALO * e) % LANES, 1)
                return fields[f][e, :, t * LANES : (t + 1) * LANES]

            for k in HALVES[half]:
                high, low = split(tile(k))
                highs.append(high)
                lows.append(low.astype(bf16))
                high, low = split(jnp.where(lane < HALO, tile(k + 1), tile(k - 1)))
                tails.append(
                    pltpu.roll(high, 16, 1) * within(8, 24)
                    + pltpu.roll(low.astype(bf16), 32, 1) * within(24, 40)
                    + pltpu.roll(high, 48, 1) * within(40, 56)
                )
        highs, lows, tails = (jnp.concatenate(parts, axis=0) for parts in (highs, lows, tails))
        data = jnp.concatenate([highs, lows, highs, tails], axis=1)
        taps = jnp.concatenate([toeplitz_of(b, e) for b in range(BASES)], axis=1)
        result = jnp.dot(data[:, 0 : taps.shape[0]], taps, preferred_element_type=f32)
        high, low = split(result)
        low = low.astype(bf16)
        for b in range(BASES):
            for i in range(4):
                rows, lanes = slice(i * ROWS, (i + 1) * ROWS), slice(b * LANES, (b + 1) * LANES)
                target[0, b, i] = high[rows, lanes]
                target[1, b, i] = low[rows, lanes]

    def finish(half, e, source):
        total = [None] * 4
        for b in range(BASES):
            high = jnp.concatenate([source[0, b, i] for i in range(4)], axis=1)
            low = jnp.concatenate([source[1, b, i] for i in range(4)], axis=1)
            smeared = jnp.dot(
                band_of(b, e),
                jnp.concatenate([high, low, high], axis=0),
                preferred_element_type=f32,
            )
            for i in range(4):
                k = HALVES[half][i % 2]
                plane = coef[e, b, :, k * LANES : (k + 1) * LANES].astype(f32)
                term = smeared[:, i * LANES : (i + 1) * LANES] * plane
                total[i] = term if total[i] is None else total[i] + term
        for i in range(2):
            weight = 1.0 / (total[2 + i] + READ_NOISE)
            val[half, e, 0, i] = weight * total[i]
            val[half, e, 1, i] = weight

    def send_halos():
        lax.fori_loop(0, EPOCHS, gather_edges, 0, unroll=4)
        pl.semaphore_wait(barrier, 2 + len(offsets))
        halo_copies = []
        for side, target in ((0, left), (1, right)):
            copy = pltpu.make_async_remote_copy(
                src_ref=pack.at[side],
                dst_ref=halo.at[side],
                send_sem=halo_send.at[side],
                recv_sem=halo_recv.at[side],
                device_id=(me, target),
                device_id_type=MESH,
            )
            copy.start()
            halo_copies.append(copy)
        return halo_copies

    buffers = (col0, col1, col2, col3)

    def step(half, n, ahead=None):
        e = 4 * n
        ahead = [(half, e + 4), (half, e + 5)] if ahead is None else ahead
        columns = [(half, e + 2), (half, e + 3), *ahead]
        for i in range(4):
            finish(half, e + i, buffers[i])
            if i < len(columns):
                spread(*columns[i], buffers[(i + 2) % 4])
        return 0

    def smear(half, start, stop):
        lax.fori_loop(start, stop, lambda n, _: step(half, n), 0)

    def select(half, index, _):
        f, i = index // (2 * SIDE), index // SIDE % 2
        rows = pl.ds(pl.multiple_of(index % SIDE * 8, 8), 8)
        values = [val[half, e, f, i, rows, :] for e in range(EPOCHS)]
        sorts = [sort_four(values[i : i + 4]) for i in range(0, EPOCHS, 4)]
        pairs = []
        for i in (0, 2):
            pairs.append(
                (
                    sort_bitonic(lower_four(sorts[i], sorts[i + 1])),
                    sort_bitonic(upper_four(sorts[i], sorts[i + 1])),
                )
            )
        low, high = merge_ends(pairs[0], pairs[1])
        for place, value in enumerate(low + high + [sum_tree(values)]):
            lists[half, place, index // SIDE, index % SIDE] = value
        return 0

    def copy_to(source, target, send, receive, dy, dx):
        copy = pltpu.make_async_remote_copy(
            src_ref=source,
            dst_ref=target,
            send_sem=send,
            recv_sem=receive,
            device_id=(peer_at(dy, dx), sky),
            device_id_type=MESH,
        )
        copy.start()
        return copy

    def send_near(half):
        copies = []
        for step in (2, 1, 3):
            x, y = (my_x + step) % SIDE, (my_y + step) % SIDE
            sems = [(near_send.at[half, i, step - 1], near_recv.at[half, i, step - 1]) for i in range(2)]
            low = copy_to(
                lists.at[half, pl.ds(0, REJECT), x], near_low.at[half, step - 1], *sems[0], 0, step
            )
            high = copy_to(
                lists.at[half, pl.ds(REJECT, REJECT + 1), :, y],
                near_high.at[half, step - 1],
                *sems[1],
                step,
                0,
            )
            copies += [low, high]
        return copies

    def tree(parts, pick):
        while len(parts) > 1:
            parts = [sort_bitonic(pick(parts[i], parts[i + 1])) for i in range(0, len(parts), 2)]
        return parts[0]

    def send_far(half, copies):
        for copy in copies:
            copy.wait_recv()
        for g in range(SIDE):
            parts = [[lists[half, i, my_x, g] for i in range(REJECT)]]
            for step in range(SIDE - 1):
                parts.append([near_low[half, step, i, g] for i in range(REJECT)])
            for i, value in enumerate(tree(parts, lower_four)):
                mid_low[half, i, g] = value
            parts = [[lists[half, REJECT + i, g, my_y] for i in range(REJECT + 1)]]
            for step in range(SIDE - 1):
                parts.append([near_high[half, step, i, g] for i in range(REJECT + 1)])
            for i, value in enumerate(tree([part[0:REJECT] for part in parts], upper_four)):
                mid_high[half, i, g] = value
            mid_high[half, REJECT, g] = sum_tree([part[REJECT] for part in parts])
        result = []
        for step in (2, 1, 3):
            x, y = (my_x + step) % SIDE, (my_y + step) % SIDE
            sems = [(far_send.at[half, i, step - 1], far_recv.at[half, i, step - 1]) for i in range(2)]
            low = copy_to(mid_low.at[half, :, y], far_low.at[half, step - 1], *sems[0], step, 0)
            high = copy_to(mid_high.at[half, :, x], far_high.at[half, step - 1], *sems[1], 0, step)
            result += [low, high]
        return result

    def send_direct(half):
        copies = []
        for i, (dy, dx) in enumerate(offsets):
            x, y = (my_x + dx) % SIDE, (my_y + dy) % SIDE
            copies.append(
                copy_to(
                    lists.at[half, :, x, y], direct.at[i], dir_send.at[i], dir_recv.at[i], dy, dx
                )
            )
        return copies

    def close_direct(half, copies):
        ends = []
        for f, pick in ((0, lower_four), (1, upper_four)):
            rows = range(f * REJECT, (f + 1) * REJECT)
            parts = [[lists[half, i, my_x, my_y] for i in rows]]
            for n, copy in enumerate(copies):
                if f == 0:
                    copy.wait_recv()
                parts.append([direct[n, i] for i in rows])
            while len(parts) > 2:
                parts = [sort_bitonic(pick(parts[i], parts[i + 1])) for i in range(0, len(parts), 2)]
            ends += pick(*parts)
        total = sum_tree(
            [lists[half, 2 * REJECT, my_x, my_y]] + [direct[n, 2 * REJECT] for n in range(len(copies))]
        )
        final[me, half] = total - sum_tree(ends)

    def close(half, copies):
        for copy in copies:
            copy.wait_recv()
        lows = [[mid_low[half, i, my_y] for i in range(REJECT)]]
        highs = [[mid_high[half, i, my_x] for i in range(REJECT + 1)]]
        for step in range(SIDE - 1):
            lows.append([far_low[half, step, i] for i in range(REJECT)])
            highs.append([far_high[half, step, i] for i in range(REJECT + 1)])
        low = lower_four(*(sort_bitonic(lower_four(lows[i], lows[i + 1])) for i in (0, 2)))
        high = upper_four(*(sort_bitonic(upper_four(highs[i], highs[i + 1])) for i in (0, 2)))
        total = sum_tree([part[REJECT] for part in highs])
        final[me, half] = total - sum_tree(low) - sum_tree(high)

    for load in portions[0]:
        load.wait()
    spread(0, 0, col0)
    spread(0, 1, col1)
    step(0, 0)
    for load in portions[1]:
        load.wait()
    halo_copies = send_halos()
    smear(0, 1, STEPS - 1)
    step(0, STEPS - 1, [])
    lax.fori_loop(0, PEERS, lambda index, _: select(0, index, _), 0, unroll=2)
    near0 = send_near(0)
    for copy in halo_copies:
        copy.wait_recv()
    for side, at_end in ((0, 0), (1, strips - 1)):
        for f in range(2):
            edge[side, f] = halo[1 - side, f] * jnp.where(sky == at_end, 0.0, 1.0)
    spread(1, 0, col0)
    spread(1, 1, col1)
    smear(1, 0, STEPS - 1)
    step(1, STEPS - 1, [])
    lax.fori_loop(0, PEERS, lambda index, _: select(1, index, _), 0, unroll=2)
    direct1 = send_direct(1)
    far0 = send_far(0, near0)
    close(0, far0)
    close_direct(1, direct1)

    copies = [
        copy_to(final.at[me], final.at[me], fin_send.at[i], fin_recv.at[i], dy, dx)
        for i, (dy, dx) in enumerate(offsets)
    ]
    for i, (dy, dx) in enumerate(offsets):
        source = peer_at(SIDE - dy, SIDE - dx)
        pltpu.make_async_remote_copy(
            src_ref=final.at[source],
            dst_ref=final.at[source],
            send_sem=fin_send.at[i],
            recv_sem=fin_recv.at[i],
            device_id=(source, sky),
            device_id_type=MESH,
        ).wait_recv()

    for half, blocks in enumerate(HALVES):
        for unit in range(PEERS):
            f, k, g = unit // (2 * SIDE), blocks[unit // SIDE % 2], unit % SIDE
            out_ref[f, 8 * g : 8 * g + 8, k * LANES : (k + 1) * LANES] = final[
                (unit % SIDE) * SIDE + unit // SIDE, half
            ]

    for copy in halo_copies + near0 + far0 + direct1 + copies:
        copy.wait_send()


def per_device(images, variances, coefficients, row_filters, col_filters, dithers):
    f32, bf16 = jnp.float32, jnp.bfloat16
    dma, vmem = pltpu.SemaphoreType.DMA, pltpu.VMEM
    tile = (OWNER_ROWS, LANES)
    trimmed = pl.pallas_call(
        kernel,
        out_shape=jax.ShapeDtypeStruct((2, ROWS, BLOCKS * LANES), f32),
        in_specs=[pl.BlockSpec(memory_space=pltpu.HBM)] * 6,
        out_specs=pl.BlockSpec(memory_space=pltpu.VMEM),
        scratch_shapes=[
            vmem((EPOCHS, ROWS, BLOCKS * LANES), f32),
            vmem((EPOCHS, ROWS, BLOCKS * LANES), f32),
            vmem((EPOCHS, BASES, ROWS, BLOCKS * LANES), bf16),
            vmem((TAPS, BASES, EPOCHS), f32),
            vmem((TAPS, BASES, EPOCHS), f32),
            pltpu.SMEM((2, EPOCHS), jnp.int32),
            vmem((LANES, LANES), f32),
            vmem((2, EPOCHS * BASES, LANES), f32),
            vmem((2, 2, ROWS, LANES), f32),
            vmem((2, 2, ROWS, LANES), f32),
            vmem((2, 2, ROWS, LANES), f32),
            vmem((2, BASES, 4, ROWS, LANES), bf16),
            vmem((2, BASES, 4, ROWS, LANES), bf16),
            vmem((2, BASES, 4, ROWS, LANES), bf16),
            vmem((2, BASES, 4, ROWS, LANES), bf16),
            vmem((2, EPOCHS, 2, 2, ROWS, LANES), f32),
            vmem((2, LISTS, SIDE, SIDE) + tile, f32),
            vmem((2, SIDE - 1, REJECT, SIDE) + tile, f32),
            vmem((2, SIDE - 1, REJECT + 1, SIDE) + tile, f32),
            vmem((2, REJECT, SIDE) + tile, f32),
            vmem((2, REJECT + 1, SIDE) + tile, f32),
            vmem((2, SIDE - 1, REJECT) + tile, f32),
            vmem((2, SIDE - 1, REJECT + 1) + tile, f32),
            vmem((PEERS - 1, LISTS) + tile, f32),
            vmem((PEERS, 2) + tile, f32),
            dma((9,)),
            dma((2,)),
            dma((2,)),
            dma((2, 2, SIDE - 1)),
            dma((2, 2, SIDE - 1)),
            dma((2, 2, SIDE - 1)),
            dma((2, 2, SIDE - 1)),
            dma((PEERS - 1,)),
            dma((PEERS - 1,)),
            dma((PEERS - 1,)),
            dma((PEERS - 1,)),
        ],
        compiler_params=pltpu.CompilerParams(
            collective_id=0, has_side_effects=True, vmem_limit_bytes=66_000_000
        ),
        name="coadd",
    )(
        images,
        variances,
        coefficients,
        jnp.transpose(row_filters, (2, 1, 0)),
        jnp.transpose(col_filters, (2, 1, 0)),
        jnp.transpose(dithers),
    )
    kept_count = float(EPOCHS * lax.axis_size("epoch") - 2 * REJECT)
    return trimmed[0] / trimmed[1], trimmed[1] / kept_count


def solution(mesh):
    placed = (
        P("epoch", None, "sky"),
        P("epoch", None, "sky"),
        P("epoch", None, None, "sky"),
        P("epoch", None, None),
        P("epoch", None, None),
        P("epoch", None),
    )
    return jax.shard_map(
        per_device,
        mesh=mesh,
        in_specs=placed,
        out_specs=(P(None, "sky"), P(None, "sky")),
        check_vma=False,
    )
```

```python
import jax
import jax.numpy as jnp
from jax import lax
from jax.experimental import pallas as pl
from jax.experimental.pallas import tpu as pltpu
from jax.sharding import PartitionSpec as P

TAPS = 11
BASES = 4
REJECT = 4
HALF = 5
HALO = 8
READ_NOISE = 0.25

LANES = 128
EPOCHS = 16
FIRST = 6
STEPS = EPOCHS // 4
ROWS = 32
BLOCKS = 4
SIDE = 4
PEERS = SIDE * SIDE
LISTS = 2 * REJECT + 1
HALVES = ((1, 2), (0, 3))
OWNER_ROWS = 8
MESH = pl.DeviceIdType.MESH


def split(value):
    high = value.astype(jnp.bfloat16)
    return high, value - high.astype(jnp.float32)


def exchange(first, second):
    return jnp.minimum(first, second), jnp.maximum(first, second)


def sort_four(values):
    a, b, c, d = values
    a, b = exchange(a, b)
    c, d = exchange(c, d)
    a, c = exchange(a, c)
    b, d = exchange(b, d)
    b, c = exchange(b, c)
    return [a, b, c, d]


def sort_bitonic(values):
    a, b, c, d = values
    a, c = exchange(a, c)
    b, d = exchange(b, d)
    a, b = exchange(a, b)
    c, d = exchange(c, d)
    return [a, b, c, d]


def lower_four(first, second):
    return [jnp.minimum(first[i], second[REJECT - 1 - i]) for i in range(REJECT)]


def upper_four(first, second):
    return [jnp.maximum(first[i], second[REJECT - 1 - i]) for i in range(REJECT)]


def merge_ends(first, second, last=False):
    low = lower_four(first[0], second[0])
    high = upper_four(first[1], second[1])
    if not last:
        low, high = sort_bitonic(low), sort_bitonic(high)
    return low, high


def sum_tree(values):
    values = list(values)
    while len(values) > 1:
        values = [values[i] + values[i + 1] for i in range(0, len(values) - 1, 2)] + (
            [values[-1]] if len(values) % 2 else []
        )
    return values[0]


def kernel(
    img_hbm, var_hbm, coef_hbm, rowf_hbm, colf_hbm, dith_hbm, out_ref,
    img, var, coef, rowf, colf, dith, filt, base, pack, halo, edge, col0, col1, col2, col3, val, lists,
    near_low, near_high, mid_low, mid_high, far_low, far_high, direct, final,
    in_sem, halo_send, halo_recv, near_send, near_recv, far_send, far_recv, dir_send, dir_recv, fin_send, fin_recv,
):
    f32, bf16 = jnp.float32, jnp.bfloat16
    me = lax.axis_index("epoch")
    sky = lax.axis_index("sky")
    strips = lax.axis_size("sky")
    my_y, my_x = me // SIDE, me % SIDE
    right, left = (sky + 1) % strips, (sky + strips - 1) % strips

    def peer_at(dy, dx):
        return ((my_y + dy) % SIDE) * SIDE + (my_x + dx) % SIDE

    offsets = [(dy, dx) for dy in (2, 1, 3, 0) for dx in (2, 1, 3, 0) if dy or dx]
    offsets.sort(key=lambda o: -(2 - abs(2 - o[0]) + 2 - abs(2 - o[1])))

    loads = [
        pltpu.make_async_copy(source, target, in_sem.at[i])
        for i, (source, target) in enumerate(((rowf_hbm, rowf), (colf_hbm, colf), (dith_hbm, dith)))
    ]
    portions = []
    for start, count in ((0, FIRST), (FIRST, EPOCHS - FIRST)):
        rows, part = pl.ds(start, count), []
        for source, target in ((img_hbm, img), (var_hbm, var), (coef_hbm, coef)):
            sem = in_sem.at[3 + 3 * len(portions) + len(part)]
            part.append(pltpu.make_async_copy(source.at[rows], target.at[rows], sem))
        portions.append(part)
    for load in loads + portions[0] + portions[1]:
        load.start()

    barrier = pltpu.get_barrier_semaphore()
    for neighbour in (left, right):
        pl.semaphore_signal(barrier, inc=1, device_id=(me, neighbour), device_id_type=MESH)
    for dy, dx in offsets:
        pl.semaphore_signal(barrier, inc=1, device_id=(peer_at(dy, dx), sky), device_id_type=MESH)

    lane = lax.broadcasted_iota(jnp.int32, (ROWS, LANES), 1)
    lane16 = lane[0:16]

    def within(start, stop, like=lane):
        return jnp.where((like >= start) & (like < stop), 1.0, 0.0).astype(bf16)

    filt[...] = jnp.zeros_like(filt)
    loads[0].wait()
    loads[1].wait()
    for j in range(TAPS):
        for b in range(BASES):
            filt[16 * b + j, 0:EPOCHS] = rowf[j, b, :]
            filt[64 + 16 * b + TAPS - 1 - j, 0:EPOCHS] = colf[j, b, :]
    turned = jnp.transpose(filt[...])[0:EPOCHS]
    for kind in range(2):
        for b in range(BASES):
            at = 16 * (BASES * kind + b)
            taps = pltpu.roll(turned, LANES - at, 1) if at else turned
            taps = jnp.where(lane16 < 16, taps, 0.0)
            high, low = split(taps)
            high, low = high.astype(f32), low.astype(bf16).astype(f32)
            if kind == 0:
                parts = high + pltpu.roll(high, ROWS, 1) + pltpu.roll(low, 2 * ROWS, 1)
            else:
                parts = high + pltpu.roll(low, 64, 1)
            base[kind, b * EPOCHS : (b + 1) * EPOCHS, :] = parts

    fields = (img, var)
    last_cols = slice((BLOCKS - 1) * LANES, BLOCKS * LANES)

    def gather_edges(e, _):
        mine = (lane >= HALO * e) & (lane < HALO * (e + 1))
        for f in range(2):
            first = pltpu.roll(fields[f][e, :, 0:LANES], HALO * e, 1)
            last = pltpu.roll(fields[f][e, :, last_cols], (HALO * e + HALO) % LANES, 1)
            pack[0, f] = jnp.where(mine, first, pack[0, f])
            pack[1, f] = jnp.where(mine, last, pack[1, f])
        return 0

    loads[2].wait()

    def filters(which, b, e):
        taps = jnp.broadcast_to(base[which, pl.ds(b * EPOCHS + e, 1), :], (16, LANES))
        return pltpu.roll(taps, 0, 1, stride=1, stride_axis=0).astype(bf16)

    near_row = []
    for g in range(2):
        apart = lane16 % ROWS - lax.broadcasted_iota(jnp.int32, (16, LANES), 0) - 16 * g
        near_row.append(jnp.where((apart <= 8) & (apart >= -8), 1.0, 0.0).astype(bf16))

    def band_of(b, e):
        taps = filters(0, b, e)
        groups = [
            pltpu.roll(taps, 8 - dith[0, e] + (16 * g - HALF - 8) % LANES, 1) * near_row[g]
            for g in range(2)
        ]
        return jnp.concatenate(groups, axis=0)[:, 0 : 3 * ROWS]

    row16 = lax.broadcasted_iota(jnp.int32, (16, LANES), 0)
    before = jnp.where((row16 >= 8) & (lane16 < 8), 1.0, 0.0).astype(bf16)
    after = jnp.where((row16 < 8) & (lane16 >= LANES - 8), 1.0, 0.0).astype(bf16)

    def toeplitz_of(b, e):
        taps = filters(1, b, e)
        turned = [pltpu.roll(taps, dith[1, e] + (16 * g - HALF) % LANES, 1) for g in range(8)]
        windows = [within(max(0, 16 * g - 8), 16 * g + 24, lane16) for g in range(8)]
        high = [turned[g] * windows[g] for g in range(8)]
        low = [turned[(g + 4) % 8] * windows[g] for g in range(8)]
        before_high, before_low = turned[7] * before, turned[3] * before
        after_high, after_low = turned[0] * after, turned[4] * after
        sides = [before_high, after_high + before_high, after_high + before_low, after_low]
        return jnp.concatenate(high + high + low + sides, axis=0)

    def spread(half, e, target):
        highs, lows, tails = [], [], []
        for f in range(2):

            def tile(t):
                if t < 0:
                    return pltpu.roll(edge[0, f], (2 * LANES - HALO - HALO * e) % LANES, 1)
                if t == BLOCKS:
                    return pltpu.roll(edge[1, f], (LANES - HALO * e) % LANES, 1)
                return fields[f][e, :, t * LANES : (t + 1) * LANES]

            for k in HALVES[half]:
                high, low = split(tile(k))
                highs.append(high)
                lows.append(low.astype(bf16))
                high, low = split(jnp.where(lane < HALO, tile(k + 1), tile(k - 1)))
                tails.append(
                    pltpu.roll(high, 16, 1) * within(8, 24)
                    + pltpu.roll(low.astype(bf16), 32, 1) * within(24, 40)
                    + pltpu.roll(high, 48, 1) * within(40, 56)
                )
        highs, lows, tails = (jnp.concatenate(parts, axis=0) for parts in (highs, lows, tails))
        data = jnp.concatenate([highs, lows, highs, tails], axis=1)
        taps = jnp.concatenate([toeplitz_of(b, e) for b in range(BASES)], axis=1)
        result = jnp.dot(data[:, 0 : taps.shape[0]], taps, preferred_element_type=f32)
        high, low = split(result)
        low = low.astype(bf16)
        for b in range(BASES):
            for i in range(4):
                rows, lanes = slice(i * ROWS, (i + 1) * ROWS), slice(b * LANES, (b + 1) * LANES)
                target[0, b, i] = high[rows, lanes]
                target[1, b, i] = low[rows, lanes]

    def finish(half, e, source):
        total = [None] * 4
        for b in range(BASES):
            high = jnp.concatenate([source[0, b, i] for i in range(4)], axis=1)
            low = jnp.concatenate([source[1, b, i] for i in range(4)], axis=1)
            smeared = jnp.dot(
                band_of(b, e),
                jnp.concatenate([high, low, high], axis=0),
                preferred_element_type=f32,
            )
            for i in range(4):
                k = HALVES[half][i % 2]
                plane = coef[e, b, :, k * LANES : (k + 1) * LANES].astype(f32)
                term = smeared[:, i * LANES : (i + 1) * LANES] * plane
                total[i] = term if total[i] is None else total[i] + term
        for i in range(2):
            weight = 1.0 / (total[2 + i] + READ_NOISE)
            val[half, e, 0, i] = weight * total[i]
            val[half, e, 1, i] = weight

    def send_halos():
        lax.fori_loop(0, EPOCHS, gather_edges, 0, unroll=16)
        pl.semaphore_wait(barrier, 2 + len(offsets))
        halo_copies = []
        for side, target in ((0, left), (1, right)):
            copy = pltpu.make_async_remote_copy(
                src_ref=pack.at[side],
                dst_ref=halo.at[side],
                send_sem=halo_send.at[side],
                recv_sem=halo_recv.at[side],
                device_id=(me, target),
                device_id_type=MESH,
            )
            copy.start()
            halo_copies.append(copy)
        return halo_copies

    buffers = (col0, col1, col2, col3)

    def step(half, n, ahead=None):
        e = 4 * n
        ahead = [(half, e + 4), (half, e + 5)] if ahead is None else ahead
        columns = [(half, e + 2), (half, e + 3), *ahead]
        for i in range(4):
            finish(half, e + i, buffers[i])
            if i < len(columns):
                spread(*columns[i], buffers[(i + 2) % 4])
        return 0

    def smear(half, start, stop):
        lax.fori_loop(start, stop, lambda n, _: step(half, n), 0)

    def select(half, index, _):
        f, i = index // (2 * SIDE), index // SIDE % 2
        rows = pl.ds(pl.multiple_of(index % SIDE * 8, 8), 8)
        values = [val[half, e, f, i, rows, :] for e in range(EPOCHS)]
        sorts = [sort_four(values[i : i + 4]) for i in range(0, EPOCHS, 4)]
        pairs = []
        for i in (0, 2):
            pairs.append(
                (
                    sort_bitonic(lower_four(sorts[i], sorts[i + 1])),
                    sort_bitonic(upper_four(sorts[i], sorts[i + 1])),
                )
            )
        low, high = merge_ends(pairs[0], pairs[1])
        for place, value in enumerate(low + high + [sum_tree(values)]):
            lists[half, place, index // SIDE, index % SIDE] = value
        return 0

    def copy_to(source, target, send, receive, dy, dx):
        copy = pltpu.make_async_remote_copy(
            src_ref=source,
            dst_ref=target,
            send_sem=send,
            recv_sem=receive,
            device_id=(peer_at(dy, dx), sky),
            device_id_type=MESH,
        )
        copy.start()
        return copy

    def send_near(half):
        copies = []
        for step in (2, 1, 3):
            x, y = (my_x + step) % SIDE, (my_y + step) % SIDE
            sems = [(near_send.at[half, i, step - 1], near_recv.at[half, i, step - 1]) for i in range(2)]
            low = copy_to(
                lists.at[half, pl.ds(0, REJECT), x], near_low.at[half, step - 1], *sems[0], 0, step
            )
            high = copy_to(
                lists.at[half, pl.ds(REJECT, REJECT + 1), :, y],
                near_high.at[half, step - 1],
                *sems[1],
                step,
                0,
            )
            copies += [low, high]
        return copies

    def tree(parts, pick):
        while len(parts) > 1:
            parts = [sort_bitonic(pick(parts[i], parts[i + 1])) for i in range(0, len(parts), 2)]
        return parts[0]

    def send_far(half, copies):
        for copy in copies:
            copy.wait_recv()
        for g in range(SIDE):
            parts = [[lists[half, i, my_x, g] for i in range(REJECT)]]
            for step in range(SIDE - 1):
                parts.append([near_low[half, step, i, g] for i in range(REJECT)])
            for i, value in enumerate(tree(parts, lower_four)):
                mid_low[half, i, g] = value
            parts = [[lists[half, REJECT + i, g, my_y] for i in range(REJECT + 1)]]
            for step in range(SIDE - 1):
                parts.append([near_high[half, step, i, g] for i in range(REJECT + 1)])
            for i, value in enumerate(tree([part[0:REJECT] for part in parts], upper_four)):
                mid_high[half, i, g] = value
            mid_high[half, REJECT, g] = sum_tree([part[REJECT] for part in parts])
        result = []
        for step in (2, 1, 3):
            x, y = (my_x + step) % SIDE, (my_y + step) % SIDE
            sems = [(far_send.at[half, i, step - 1], far_recv.at[half, i, step - 1]) for i in range(2)]
            low = copy_to(mid_low.at[half, :, y], far_low.at[half, step - 1], *sems[0], step, 0)
            high = copy_to(mid_high.at[half, :, x], far_high.at[half, step - 1], *sems[1], 0, step)
            result += [low, high]
        return result

    def send_direct(half):
        copies = []
        for i, (dy, dx) in enumerate(offsets):
            x, y = (my_x + dx) % SIDE, (my_y + dy) % SIDE
            copies.append(
                copy_to(
                    lists.at[half, :, x, y], direct.at[i], dir_send.at[i], dir_recv.at[i], dy, dx
                )
            )
        return copies

    def close_direct(half, copies):
        ends = []
        for f, pick in ((0, lower_four), (1, upper_four)):
            rows = range(f * REJECT, (f + 1) * REJECT)
            parts = [[lists[half, i, my_x, my_y] for i in rows]]
            for n, copy in enumerate(copies):
                if f == 0:
                    copy.wait_recv()
                parts.append([direct[n, i] for i in rows])
            while len(parts) > 2:
                parts = [sort_bitonic(pick(parts[i], parts[i + 1])) for i in range(0, len(parts), 2)]
            ends += pick(*parts)
        total = sum_tree(
            [lists[half, 2 * REJECT, my_x, my_y]] + [direct[n, 2 * REJECT] for n in range(len(copies))]
        )
        final[me, half] = total - sum_tree(ends)

    def close(half, copies):
        for copy in copies:
            copy.wait_recv()
        lows = [[mid_low[half, i, my_y] for i in range(REJECT)]]
        highs = [[mid_high[half, i, my_x] for i in range(REJECT + 1)]]
        for step in range(SIDE - 1):
            lows.append([far_low[half, step, i] for i in range(REJECT)])
            highs.append([far_high[half, step, i] for i in range(REJECT + 1)])
        low = lower_four(*(sort_bitonic(lower_four(lows[i], lows[i + 1])) for i in (0, 2)))
        high = upper_four(*(sort_bitonic(upper_four(highs[i], highs[i + 1])) for i in (0, 2)))
        total = sum_tree([part[REJECT] for part in highs])
        final[me, half] = total - sum_tree(low) - sum_tree(high)

    for load in portions[0]:
        load.wait()
    spread(0, 0, col0)
    spread(0, 1, col1)
    step(0, 0)
    for load in portions[1]:
        load.wait()
    halo_copies = send_halos()
    smear(0, 1, STEPS - 1)
    step(0, STEPS - 1, [])
    lax.fori_loop(0, PEERS, lambda index, _: select(0, index, _), 0, unroll=4)
    near0 = send_near(0)
    for copy in halo_copies:
        copy.wait_recv()
    for side, at_end in ((0, 0), (1, strips - 1)):
        for f in range(2):
            edge[side, f] = halo[1 - side, f] * jnp.where(sky == at_end, 0.0, 1.0)
    spread(1, 0, col0)
    spread(1, 1, col1)
    smear(1, 0, STEPS - 1)
    step(1, STEPS - 1, [])
    lax.fori_loop(0, PEERS, lambda index, _: select(1, index, _), 0, unroll=4)
    direct1 = send_direct(1)
    far0 = send_far(0, near0)
    close(0, far0)
    close_direct(1, direct1)

    copies = [
        copy_to(final.at[me], final.at[me], fin_send.at[i], fin_recv.at[i], dy, dx)
        for i, (dy, dx) in enumerate(offsets)
    ]
    for i, (dy, dx) in enumerate(offsets):
        source = peer_at(SIDE - dy, SIDE - dx)
        pltpu.make_async_remote_copy(
            src_ref=final.at[source],
            dst_ref=final.at[source],
            send_sem=fin_send.at[i],
            recv_sem=fin_recv.at[i],
            device_id=(source, sky),
            device_id_type=MESH,
        ).wait_recv()

    for half, blocks in enumerate(HALVES):
        for unit in range(PEERS):
            f, k, g = unit // (2 * SIDE), blocks[unit // SIDE % 2], unit % SIDE
            out_ref[f, 8 * g : 8 * g + 8, k * LANES : (k + 1) * LANES] = final[
                (unit % SIDE) * SIDE + unit // SIDE, half
            ]

    for copy in halo_copies + near0 + far0 + direct1 + copies:
        copy.wait_send()


def per_device(images, variances, coefficients, row_filters, col_filters, dithers):
    f32, bf16 = jnp.float32, jnp.bfloat16
    dma, vmem = pltpu.SemaphoreType.DMA, pltpu.VMEM
    tile = (OWNER_ROWS, LANES)
    trimmed = pl.pallas_call(
        kernel,
        out_shape=jax.ShapeDtypeStruct((2, ROWS, BLOCKS * LANES), f32),
        in_specs=[pl.BlockSpec(memory_space=pltpu.HBM)] * 6,
        out_specs=pl.BlockSpec(memory_space=pltpu.VMEM),
        scratch_shapes=[
            vmem((EPOCHS, ROWS, BLOCKS * LANES), f32),
            vmem((EPOCHS, ROWS, BLOCKS * LANES), f32),
            vmem((EPOCHS, BASES, ROWS, BLOCKS * LANES), bf16),
            vmem((TAPS, BASES, EPOCHS), f32),
            vmem((TAPS, BASES, EPOCHS), f32),
            pltpu.SMEM((2, EPOCHS), jnp.int32),
            vmem((LANES, LANES), f32),
            vmem((2, EPOCHS * BASES, LANES), f32),
            vmem((2, 2, ROWS, LANES), f32),
            vmem((2, 2, ROWS, LANES), f32),
            vmem((2, 2, ROWS, LANES), f32),
            vmem((2, BASES, 4, ROWS, LANES), bf16),
            vmem((2, BASES, 4, ROWS, LANES), bf16),
            vmem((2, BASES, 4, ROWS, LANES), bf16),
            vmem((2, BASES, 4, ROWS, LANES), bf16),
            vmem((2, EPOCHS, 2, 2, ROWS, LANES), f32),
            vmem((2, LISTS, SIDE, SIDE) + tile, f32),
            vmem((2, SIDE - 1, REJECT, SIDE) + tile, f32),
            vmem((2, SIDE - 1, REJECT + 1, SIDE) + tile, f32),
            vmem((2, REJECT, SIDE) + tile, f32),
            vmem((2, REJECT + 1, SIDE) + tile, f32),
            vmem((2, SIDE - 1, REJECT) + tile, f32),
            vmem((2, SIDE - 1, REJECT + 1) + tile, f32),
            vmem((PEERS - 1, LISTS) + tile, f32),
            vmem((PEERS, 2) + tile, f32),
            dma((9,)),
            dma((2,)),
            dma((2,)),
            dma((2, 2, SIDE - 1)),
            dma((2, 2, SIDE - 1)),
            dma((2, 2, SIDE - 1)),
            dma((2, 2, SIDE - 1)),
            dma((PEERS - 1,)),
            dma((PEERS - 1,)),
            dma((PEERS - 1,)),
            dma((PEERS - 1,)),
        ],
        compiler_params=pltpu.CompilerParams(
            collective_id=0, has_side_effects=True, vmem_limit_bytes=66_000_000
        ),
        name="coadd",
    )(
        images,
        variances,
        coefficients,
        jnp.transpose(row_filters, (2, 1, 0)),
        jnp.transpose(col_filters, (2, 1, 0)),
        jnp.transpose(dithers),
    )
    kept_count = float(EPOCHS * lax.axis_size("epoch") - 2 * REJECT)
    return trimmed[0] / trimmed[1], trimmed[1] / kept_count


def solution(mesh):
    placed = (
        P("epoch", None, "sky"),
        P("epoch", None, "sky"),
        P("epoch", None, None, "sky"),
        P("epoch", None, None),
        P("epoch", None, None),
        P("epoch", None),
    )
    return jax.shard_map(
        per_device,
        mesh=mesh,
        in_specs=placed,
        out_specs=(P(None, "sky"), P(None, "sky")),
        check_vma=False,
    )
```

```python
import jax
import jax.numpy as jnp
from jax import lax
from jax.experimental import pallas as pl
from jax.experimental.pallas import tpu as pltpu
from jax.sharding import PartitionSpec as P

TAPS = 11
BASES = 4
REJECT = 4
HALF = 5
HALO = 8
READ_NOISE = 0.25

LANES = 128
EPOCHS = 16
FIRST = 6
STEPS = EPOCHS // 4
ROWS = 32
BLOCKS = 4
SIDE = 4
PEERS = SIDE * SIDE
LISTS = 2 * REJECT + 1
HALVES = ((1, 2), (0, 3))
OWNER_ROWS = 8
MESH = pl.DeviceIdType.MESH


def split(value):
    high = value.astype(jnp.bfloat16)
    return high, value - high.astype(jnp.float32)


def exchange(first, second):
    return jnp.minimum(first, second), jnp.maximum(first, second)


def sort_four(values):
    a, b, c, d = values
    a, b = exchange(a, b)
    c, d = exchange(c, d)
    a, c = exchange(a, c)
    b, d = exchange(b, d)
    b, c = exchange(b, c)
    return [a, b, c, d]


def sort_bitonic(values):
    a, b, c, d = values
    a, c = exchange(a, c)
    b, d = exchange(b, d)
    a, b = exchange(a, b)
    c, d = exchange(c, d)
    return [a, b, c, d]


def lower_four(first, second):
    return [jnp.minimum(first[i], second[REJECT - 1 - i]) for i in range(REJECT)]


def upper_four(first, second):
    return [jnp.maximum(first[i], second[REJECT - 1 - i]) for i in range(REJECT)]


def merge_ends(first, second, last=False):
    low = lower_four(first[0], second[0])
    high = upper_four(first[1], second[1])
    if not last:
        low, high = sort_bitonic(low), sort_bitonic(high)
    return low, high


def sum_tree(values):
    values = list(values)
    while len(values) > 1:
        values = [values[i] + values[i + 1] for i in range(0, len(values) - 1, 2)] + (
            [values[-1]] if len(values) % 2 else []
        )
    return values[0]


def kernel(
    img_hbm, var_hbm, coef_hbm, rowf_hbm, colf_hbm, dith_hbm, out_ref,
    img, var, coef, rowf, colf, dith, filt, base, pack, halo, edge, col0, col1, col2, col3, val, lists,
    near_low, near_high, mid_low, mid_high, far_low, far_high, direct, final,
    in_sem, halo_send, halo_recv, near_send, near_recv, far_send, far_recv, dir_send, dir_recv, fin_send, fin_recv,
):
    f32, bf16 = jnp.float32, jnp.bfloat16
    me = lax.axis_index("epoch")
    sky = lax.axis_index("sky")
    strips = lax.axis_size("sky")
    my_y, my_x = me // SIDE, me % SIDE
    right, left = (sky + 1) % strips, (sky + strips - 1) % strips

    def peer_at(dy, dx):
        return ((my_y + dy) % SIDE) * SIDE + (my_x + dx) % SIDE

    offsets = [(dy, dx) for dy in (2, 1, 3, 0) for dx in (2, 1, 3, 0) if dy or dx]
    offsets.sort(key=lambda o: -(2 - abs(2 - o[0]) + 2 - abs(2 - o[1])))

    loads = [
        pltpu.make_async_copy(source, target, in_sem.at[i])
        for i, (source, target) in enumerate(((rowf_hbm, rowf), (colf_hbm, colf), (dith_hbm, dith)))
    ]
    portions = []
    for start, count in ((0, FIRST), (FIRST, EPOCHS - FIRST)):
        rows, part = pl.ds(start, count), []
        for source, target in ((img_hbm, img), (var_hbm, var), (coef_hbm, coef)):
            sem = in_sem.at[3 + 3 * len(portions) + len(part)]
            part.append(pltpu.make_async_copy(source.at[rows], target.at[rows], sem))
        portions.append(part)
    for load in loads + portions[0] + portions[1]:
        load.start()

    barrier = pltpu.get_barrier_semaphore()
    for neighbour in (left, right):
        pl.semaphore_signal(barrier, inc=1, device_id=(me, neighbour), device_id_type=MESH)
    for dy, dx in offsets:
        pl.semaphore_signal(barrier, inc=1, device_id=(peer_at(dy, dx), sky), device_id_type=MESH)

    lane = lax.broadcasted_iota(jnp.int32, (ROWS, LANES), 1)
    lane16 = lane[0:16]

    def within(start, stop, like=lane):
        return jnp.where((like >= start) & (like < stop), 1.0, 0.0).astype(bf16)

    filt[...] = jnp.zeros_like(filt)
    loads[0].wait()
    loads[1].wait()
    for j in range(TAPS):
        for b in range(BASES):
            filt[16 * b + j, 0:EPOCHS] = rowf[j, b, :]
            filt[64 + 16 * b + TAPS - 1 - j, 0:EPOCHS] = colf[j, b, :]
    turned = jnp.transpose(filt[...])[0:EPOCHS]
    for kind in range(2):
        for b in range(BASES):
            at = 16 * (BASES * kind + b)
            taps = pltpu.roll(turned, LANES - at, 1) if at else turned
            taps = jnp.where(lane16 < 16, taps, 0.0)
            high, low = split(taps)
            high, low = high.astype(f32), low.astype(bf16).astype(f32)
            if kind == 0:
                parts = high + pltpu.roll(high, ROWS, 1) + pltpu.roll(low, 2 * ROWS, 1)
            else:
                parts = high + pltpu.roll(low, 64, 1)
            base[kind, b * EPOCHS : (b + 1) * EPOCHS, :] = parts

    fields = (img, var)
    last_cols = slice((BLOCKS - 1) * LANES, BLOCKS * LANES)

    def gather_edges(e, _):
        mine = (lane >= HALO * e) & (lane < HALO * (e + 1))
        for f in range(2):
            first = pltpu.roll(fields[f][e, :, 0:LANES], HALO * e, 1)
            last = pltpu.roll(fields[f][e, :, last_cols], (HALO * e + HALO) % LANES, 1)
            pack[0, f] = jnp.where(mine, first, pack[0, f])
            pack[1, f] = jnp.where(mine, last, pack[1, f])
        return 0

    loads[2].wait()

    def filters(which, b, e):
        taps = jnp.broadcast_to(base[which, pl.ds(b * EPOCHS + e, 1), :], (16, LANES))
        return pltpu.roll(taps, 0, 1, stride=1, stride_axis=0).astype(bf16)

    near_row = []
    for g in range(2):
        apart = lane16 % ROWS - lax.broadcasted_iota(jnp.int32, (16, LANES), 0) - 16 * g
        near_row.append(jnp.where((apart <= 8) & (apart >= -8), 1.0, 0.0).astype(bf16))

    def band_of(b, e):
        taps = filters(0, b, e)
        groups = [
            pltpu.roll(taps, 8 - dith[0, e] + (16 * g - HALF - 8) % LANES, 1) * near_row[g]
            for g in range(2)
        ]
        return jnp.concatenate(groups, axis=0)[:, 0 : 3 * ROWS]

    row16 = lax.broadcasted_iota(jnp.int32, (16, LANES), 0)
    before = jnp.where((row16 >= 8) & (lane16 < 8), 1.0, 0.0).astype(bf16)
    after = jnp.where((row16 < 8) & (lane16 >= LANES - 8), 1.0, 0.0).astype(bf16)

    def toeplitz_of(b, e):
        taps = filters(1, b, e)
        turned = [pltpu.roll(taps, dith[1, e] + (16 * g - HALF) % LANES, 1) for g in range(8)]
        windows = [within(max(0, 16 * g - 8), 16 * g + 24, lane16) for g in range(8)]
        high = [turned[g] * windows[g] for g in range(8)]
        low = [turned[(g + 4) % 8] * windows[g] for g in range(8)]
        before_high, before_low = turned[7] * before, turned[3] * before
        after_high, after_low = turned[0] * after, turned[4] * after
        sides = [before_high, after_high + before_high, after_high + before_low, after_low]
        return jnp.concatenate(high + high + low + sides, axis=0)

    def spread(half, e, target):
        highs, lows, tails = [], [], []
        for f in range(2):

            def tile(t):
                if t < 0:
                    return pltpu.roll(edge[0, f], (2 * LANES - HALO - HALO * e) % LANES, 1)
                if t == BLOCKS:
                    return pltpu.roll(edge[1, f], (LANES - HALO * e) % LANES, 1)
                return fields[f][e, :, t * LANES : (t + 1) * LANES]

            for k in HALVES[half]:
                high, low = split(tile(k))
                highs.append(high)
                lows.append(low.astype(bf16))
                high, low = split(jnp.where(lane < HALO, tile(k + 1), tile(k - 1)))
                tails.append(
                    pltpu.roll(high, 16, 1) * within(8, 24)
                    + pltpu.roll(low.astype(bf16), 32, 1) * within(24, 40)
                    + pltpu.roll(high, 48, 1) * within(40, 56)
                )
        highs, lows, tails = (jnp.concatenate(parts, axis=0) for parts in (highs, lows, tails))
        data = jnp.concatenate([highs, lows, highs, tails], axis=1)
        taps = jnp.concatenate([toeplitz_of(b, e) for b in range(BASES)], axis=1)
        result = jnp.dot(data[:, 0 : taps.shape[0]], taps, preferred_element_type=f32)
        high, low = split(result)
        low = low.astype(bf16)
        for b in range(BASES):
            for i in range(4):
                rows, lanes = slice(i * ROWS, (i + 1) * ROWS), slice(b * LANES, (b + 1) * LANES)
                target[0, b, i] = high[rows, lanes]
                target[1, b, i] = low[rows, lanes]

    def finish(half, e, source):
        total = [None] * 4
        for b in range(BASES):
            high = jnp.concatenate([source[0, b, i] for i in range(4)], axis=1)
            low = jnp.concatenate([source[1, b, i] for i in range(4)], axis=1)
            smeared = jnp.dot(
                band_of(b, e),
                jnp.concatenate([high, low, high], axis=0),
                preferred_element_type=f32,
            )
            for i in range(4):
                k = HALVES[half][i % 2]
                plane = coef[e, b, :, k * LANES : (k + 1) * LANES].astype(f32)
                term = smeared[:, i * LANES : (i + 1) * LANES] * plane
                total[i] = term if total[i] is None else total[i] + term
        for i in range(2):
            weight = 1.0 / (total[2 + i] + READ_NOISE)
            val[half, e, 0, i] = weight * total[i]
            val[half, e, 1, i] = weight

    def send_halos():
        lax.fori_loop(0, EPOCHS, gather_edges, 0, unroll=16)
        pl.semaphore_wait(barrier, 2 + len(offsets))
        halo_copies = []
        for side, target in ((0, left), (1, right)):
            copy = pltpu.make_async_remote_copy(
                src_ref=pack.at[side],
                dst_ref=halo.at[side],
                send_sem=halo_send.at[side],
                recv_sem=halo_recv.at[side],
                device_id=(me, target),
                device_id_type=MESH,
            )
            copy.start()
            halo_copies.append(copy)
        return halo_copies

    buffers = (col0, col1, col2, col3)

    def step(half, n, ahead=None):
        e = 4 * n
        ahead = [(half, e + 4), (half, e + 5)] if ahead is None else ahead
        columns = [(half, e + 2), (half, e + 3), *ahead]
        for i in range(4):
            finish(half, e + i, buffers[i])
            if i < len(columns):
                spread(*columns[i], buffers[(i + 2) % 4])
        return 0

    def smear(half, start, stop):
        lax.fori_loop(start, stop, lambda n, _: step(half, n), 0)

    def select(half, index, _):
        f, i = index // (2 * SIDE), index // SIDE % 2
        rows = pl.ds(pl.multiple_of(index % SIDE * 8, 8), 8)
        values = [val[half, e, f, i, rows, :] for e in range(EPOCHS)]
        sorts = [sort_four(values[i : i + 4]) for i in range(0, EPOCHS, 4)]
        pairs = []
        for i in (0, 2):
            pairs.append(
                (
                    sort_bitonic(lower_four(sorts[i], sorts[i + 1])),
                    sort_bitonic(upper_four(sorts[i], sorts[i + 1])),
                )
            )
        low, high = merge_ends(pairs[0], pairs[1])
        for place, value in enumerate(low + high + [sum_tree(values)]):
            lists[half, place, index // SIDE, index % SIDE] = value
        return 0

    def copy_to(source, target, send, receive, dy, dx):
        copy = pltpu.make_async_remote_copy(
            src_ref=source,
            dst_ref=target,
            send_sem=send,
            recv_sem=receive,
            device_id=(peer_at(dy, dx), sky),
            device_id_type=MESH,
        )
        copy.start()
        return copy

    def send_near(half):
        copies = []
        for step in (2, 1, 3):
            x, y = (my_x + step) % SIDE, (my_y + step) % SIDE
            sems = [(near_send.at[half, i, step - 1], near_recv.at[half, i, step - 1]) for i in range(2)]
            low = copy_to(
                lists.at[half, pl.ds(0, REJECT), x], near_low.at[half, step - 1], *sems[0], 0, step
            )
            high = copy_to(
                lists.at[half, pl.ds(REJECT, REJECT + 1), :, y],
                near_high.at[half, step - 1],
                *sems[1],
                step,
                0,
            )
            copies += [low, high]
        return copies

    def tree(parts, pick):
        while len(parts) > 1:
            parts = [sort_bitonic(pick(parts[i], parts[i + 1])) for i in range(0, len(parts), 2)]
        return parts[0]

    def send_far(half, copies):
        for copy in copies:
            copy.wait_recv()
        for g in range(SIDE):
            parts = [[lists[half, i, my_x, g] for i in range(REJECT)]]
            for step in range(SIDE - 1):
                parts.append([near_low[half, step, i, g] for i in range(REJECT)])
            for i, value in enumerate(tree(parts, lower_four)):
                mid_low[half, i, g] = value
            parts = [[lists[half, REJECT + i, g, my_y] for i in range(REJECT + 1)]]
            for step in range(SIDE - 1):
                parts.append([near_high[half, step, i, g] for i in range(REJECT + 1)])
            for i, value in enumerate(tree([part[0:REJECT] for part in parts], upper_four)):
                mid_high[half, i, g] = value
            mid_high[half, REJECT, g] = sum_tree([part[REJECT] for part in parts])
        result = []
        for step in (2, 1, 3):
            x, y = (my_x + step) % SIDE, (my_y + step) % SIDE
            sems = [(far_send.at[half, i, step - 1], far_recv.at[half, i, step - 1]) for i in range(2)]
            low = copy_to(mid_low.at[half, :, y], far_low.at[half, step - 1], *sems[0], step, 0)
            high = copy_to(mid_high.at[half, :, x], far_high.at[half, step - 1], *sems[1], 0, step)
            result += [low, high]
        return result

    def send_direct(half):
        copies = []
        for i, (dy, dx) in enumerate(offsets):
            x, y = (my_x + dx) % SIDE, (my_y + dy) % SIDE
            copies.append(
                copy_to(
                    lists.at[half, :, x, y], direct.at[i], dir_send.at[i], dir_recv.at[i], dy, dx
                )
            )
        return copies

    def close_direct(half, copies):
        def listed(n, start, count):
            if n < 0:
                return [lists[half, i, my_x, my_y] for i in range(start, start + count)]
            return [direct[n, i] for i in range(start, start + count)]

        lows, highs, sums = [], [], []
        for start in range(0, PEERS, SIDE):
            group = [n if n < len(copies) else -1 for n in range(start, start + SIDE)]
            for n in group:
                if n >= 0:
                    copies[n].wait_recv()
            lows.append(tree([listed(n, 0, REJECT) for n in group], lower_four))
            highs.append(tree([listed(n, REJECT, REJECT) for n in group], upper_four))
            sums.append(sum_tree([listed(n, 2 * REJECT, 1)[0] for n in group]))
        low = lower_four(*(sort_bitonic(lower_four(lows[i], lows[i + 1])) for i in (0, 2)))
        high = upper_four(*(sort_bitonic(upper_four(highs[i], highs[i + 1])) for i in (0, 2)))
        total, ends = sum_tree(sums), low + high
        final[me, half] = total - sum_tree(ends)

    def close(half, copies):
        for copy in copies:
            copy.wait_recv()
        lows = [[mid_low[half, i, my_y] for i in range(REJECT)]]
        highs = [[mid_high[half, i, my_x] for i in range(REJECT + 1)]]
        for step in range(SIDE - 1):
            lows.append([far_low[half, step, i] for i in range(REJECT)])
            highs.append([far_high[half, step, i] for i in range(REJECT + 1)])
        low = lower_four(*(sort_bitonic(lower_four(lows[i], lows[i + 1])) for i in (0, 2)))
        high = upper_four(*(sort_bitonic(upper_four(highs[i], highs[i + 1])) for i in (0, 2)))
        total = sum_tree([part[REJECT] for part in highs])
        final[me, half] = total - sum_tree(low) - sum_tree(high)

    for load in portions[0]:
        load.wait()
    spread(0, 0, col0)
    spread(0, 1, col1)
    step(0, 0)
    for load in portions[1]:
        load.wait()
    halo_copies = send_halos()
    smear(0, 1, STEPS - 1)
    step(0, STEPS - 1, [])
    lax.fori_loop(0, PEERS, lambda index, _: select(0, index, _), 0, unroll=4)
    near0 = send_near(0)
    for copy in halo_copies:
        copy.wait_recv()
    for side, at_end in ((0, 0), (1, strips - 1)):
        for f in range(2):
            edge[side, f] = halo[1 - side, f] * jnp.where(sky == at_end, 0.0, 1.0)
    spread(1, 0, col0)
    spread(1, 1, col1)
    smear(1, 0, STEPS - 1)
    step(1, STEPS - 1, [])
    lax.fori_loop(0, PEERS, lambda index, _: select(1, index, _), 0, unroll=4)
    direct1 = send_direct(1)
    far0 = send_far(0, near0)
    close(0, far0)
    close_direct(1, direct1)

    copies = [
        copy_to(final.at[me], final.at[me], fin_send.at[i], fin_recv.at[i], dy, dx)
        for i, (dy, dx) in enumerate(offsets)
    ]
    for i, (dy, dx) in enumerate(offsets):
        source = peer_at(SIDE - dy, SIDE - dx)
        pltpu.make_async_remote_copy(
            src_ref=final.at[source],
            dst_ref=final.at[source],
            send_sem=fin_send.at[i],
            recv_sem=fin_recv.at[i],
            device_id=(source, sky),
            device_id_type=MESH,
        ).wait_recv()

    for half, blocks in enumerate(HALVES):
        for unit in range(PEERS):
            f, k, g = unit // (2 * SIDE), blocks[unit // SIDE % 2], unit % SIDE
            out_ref[f, 8 * g : 8 * g + 8, k * LANES : (k + 1) * LANES] = final[
                (unit % SIDE) * SIDE + unit // SIDE, half
            ]

    for copy in halo_copies + near0 + far0 + direct1 + copies:
        copy.wait_send()


def per_device(images, variances, coefficients, row_filters, col_filters, dithers):
    f32, bf16 = jnp.float32, jnp.bfloat16
    dma, vmem = pltpu.SemaphoreType.DMA, pltpu.VMEM
    tile = (OWNER_ROWS, LANES)
    trimmed = pl.pallas_call(
        kernel,
        out_shape=jax.ShapeDtypeStruct((2, ROWS, BLOCKS * LANES), f32),
        in_specs=[pl.BlockSpec(memory_space=pltpu.HBM)] * 6,
        out_specs=pl.BlockSpec(memory_space=pltpu.VMEM),
        scratch_shapes=[
            vmem((EPOCHS, ROWS, BLOCKS * LANES), f32),
            vmem((EPOCHS, ROWS, BLOCKS * LANES), f32),
            vmem((EPOCHS, BASES, ROWS, BLOCKS * LANES), bf16),
            vmem((TAPS, BASES, EPOCHS), f32),
            vmem((TAPS, BASES, EPOCHS), f32),
            pltpu.SMEM((2, EPOCHS), jnp.int32),
            vmem((LANES, LANES), f32),
            vmem((2, EPOCHS * BASES, LANES), f32),
            vmem((2, 2, ROWS, LANES), f32),
            vmem((2, 2, ROWS, LANES), f32),
            vmem((2, 2, ROWS, LANES), f32),
            vmem((2, BASES, 4, ROWS, LANES), bf16),
            vmem((2, BASES, 4, ROWS, LANES), bf16),
            vmem((2, BASES, 4, ROWS, LANES), bf16),
            vmem((2, BASES, 4, ROWS, LANES), bf16),
            vmem((2, EPOCHS, 2, 2, ROWS, LANES), f32),
            vmem((2, LISTS, SIDE, SIDE) + tile, f32),
            vmem((2, SIDE - 1, REJECT, SIDE) + tile, f32),
            vmem((2, SIDE - 1, REJECT + 1, SIDE) + tile, f32),
            vmem((2, REJECT, SIDE) + tile, f32),
            vmem((2, REJECT + 1, SIDE) + tile, f32),
            vmem((2, SIDE - 1, REJECT) + tile, f32),
            vmem((2, SIDE - 1, REJECT + 1) + tile, f32),
            vmem((PEERS - 1, LISTS) + tile, f32),
            vmem((PEERS, 2) + tile, f32),
            dma((9,)),
            dma((2,)),
            dma((2,)),
            dma((2, 2, SIDE - 1)),
            dma((2, 2, SIDE - 1)),
            dma((2, 2, SIDE - 1)),
            dma((2, 2, SIDE - 1)),
            dma((PEERS - 1,)),
            dma((PEERS - 1,)),
            dma((PEERS - 1,)),
            dma((PEERS - 1,)),
        ],
        compiler_params=pltpu.CompilerParams(
            collective_id=0, has_side_effects=True, vmem_limit_bytes=66_000_000
        ),
        name="coadd",
    )(
        images,
        variances,
        coefficients,
        jnp.transpose(row_filters, (2, 1, 0)),
        jnp.transpose(col_filters, (2, 1, 0)),
        jnp.transpose(dithers),
    )
    kept_count = float(EPOCHS * lax.axis_size("epoch") - 2 * REJECT)
    return trimmed[0] / trimmed[1], trimmed[1] / kept_count


def solution(mesh):
    placed = (
        P("epoch", None, "sky"),
        P("epoch", None, "sky"),
        P("epoch", None, None, "sky"),
        P("epoch", None, None),
        P("epoch", None, None),
        P("epoch", None),
    )
    return jax.shard_map(
        per_device,
        mesh=mesh,
        in_specs=placed,
        out_specs=(P(None, "sky"), P(None, "sky")),
        check_vma=False,
    )
```
